32 devices in a mesh: seq: 8 (over y, x, core), batch: 4 (over z).
Axes of the slice: x: 2, y: 2, z: 4, core: 2. Of those that a mesh axis runs over, the one named last changes fastest.
Arguments:
- values: bfloat16 [1, 2048, 512], P(None, 'seq', 'batch'), may hold values from -6 to 6
- gate_in: bfloat16 [1, 2048, 512], P(None, 'seq', 'batch'), may hold values from -6 to 6
- gate_out: bfloat16 [1, 2048, 512], P(None, 'seq', 'batch'), may hold values from -6 to 6
- cotangent: bfloat16 [1, 2048, 512], P(None, 'seq', 'batch'), may hold values from -6 to 6
- filters: float32 [64, 2048], P(None, 'seq'), may hold values from -0.125 to 0.125
Outputs:
- grad_values: bfloat16 [1, 2048, 512], P(None, 'seq', 'batch')
- grad_gate_in: bfloat16 [1, 2048, 512], P(None, 'seq', 'batch')
- grad_gate_out: bfloat16 [1, 2048, 512], P(None, 'seq', 'batch')
- grad_filters: float32 [64, 2048], P('batch', 'seq')
The draws below stay inside these ranges and needn't reach their ends.
All inputs are finite; a program needn't handle non-finite values.
Results may differ from the reference program's by a relative error of at most 0.012.
Values may be sent and summed in bfloat16 or wider, within the bound.
A program may use at most 128 MiB of HBM per device.

```python
import jax
import jax.numpy as jnp
from jax import lax

CHANNELS = 512
FILTERS = 64
SEQS = 1
SEQ_LEN = 2048


def steps_of(key, dims, split, least, high):
    factor_of, own = 1.0, jax.random.fold_in(key, 6)
    for axis_at, parts in split:
        heights = jnp.exp(jax.random.uniform(jax.random.fold_in(own, axis_at), (parts,), jnp.float32, least / len(split), high / len(split)))
        factor_of = factor_of * jnp.repeat(heights, dims[axis_at] // parts).reshape([-1 if axis == axis_at else 1 for axis in range(len(dims))])
    return factor_of


def noise(key, extent, width, most, shards=(), kind=jnp.bfloat16):
    drawn = width * jax.random.normal(key, extent, jnp.float32)
    if shards:
        drawn = drawn * steps_of(key, extent, shards, -0.22, 0.18)
    return jnp.clip(drawn, -most, most).astype(kind)


def setup_inputs(seed: int = 0) -> dict:
    keys = jax.random.split(jax.random.key(seed), 6)
    values = noise(keys[0], (SEQS, SEQ_LEN, CHANNELS), 1.0, 6.0, ((1, 8), (2, 4)))
    gate_in = noise(keys[1], (SEQS, SEQ_LEN, CHANNELS), 1.0, 6.0, ((1, 8), (2, 4)))
    gate_out = noise(keys[2], (SEQS, SEQ_LEN, CHANNELS), 1.0, 6.0, ((1, 8), (2, 4)))
    cotangent = noise(keys[3], (SEQS, SEQ_LEN, CHANNELS), 1.0, 6.0, ((1, 8), (2, 4)))
    filters = noise(keys[4], (FILTERS, SEQ_LEN), SEQ_LEN ** -0.5, 0.125, ((1, 8),), jnp.float32)
    return {"values": values, "gate_in": gate_in, "gate_out": gate_out, "cotangent": cotangent, "filters": filters}


def reference(values, gate_in, gate_out, cotangent, filters):
    shared = CHANNELS // FILTERS
    padded_len = 2 * SEQ_LEN
    mixed_in = (values.astype(jnp.float32) * gate_in.astype(jnp.float32)).astype(jnp.bfloat16)
    grad_mixed = (cotangent.astype(jnp.float32) * gate_out.astype(jnp.float32)).astype(jnp.bfloat16)

    def blocks(series):
        return jnp.transpose(series.astype(jnp.float32).reshape(SEQS, SEQ_LEN, shared, FILTERS), (2, 0, 3, 1))
    spec_tap = jnp.fft.rfft(filters, n=padded_len, axis=-1)

    def block_step(tap_total, pair):
        mixed_block, grad_block = pair
        spec_in = jnp.fft.rfft(mixed_block, n=padded_len, axis=-1)
        spec_grad = jnp.fft.rfft(grad_block, n=padded_len, axis=-1)
        conv_part = jnp.fft.irfft(spec_tap * spec_in, n=padded_len, axis=-1)[..., :SEQ_LEN].astype(jnp.bfloat16)
        back_part = jnp.fft.irfft(jnp.conj(spec_tap) * spec_grad, n=padded_len, axis=-1)[..., :SEQ_LEN].astype(jnp.bfloat16)
        tap_part = jnp.fft.irfft(jnp.conj(spec_in) * spec_grad, n=padded_len, axis=-1)[..., :SEQ_LEN]
        return (tap_total + lax.optimization_barrier(jnp.sum(tap_part, axis=0)), (conv_part, back_part))
    start_total = jnp.zeros((FILTERS, SEQ_LEN), jnp.float32)
    tap_total, (conv_blocks, back_blocks) = lax.scan(block_step, start_total, (blocks(mixed_in), blocks(grad_mixed)))
    conv_seq = jnp.transpose(conv_blocks, (1, 3, 0, 2)).reshape(SEQS, SEQ_LEN, CHANNELS).astype(jnp.float32)
    back_seq = jnp.transpose(back_blocks, (1, 3, 0, 2)).reshape(SEQS, SEQ_LEN, CHANNELS).astype(jnp.float32)
    grad_values = (gate_in.astype(jnp.float32) * back_seq).astype(jnp.bfloat16)
    grad_gate_in = (values.astype(jnp.float32) * back_seq).astype(jnp.bfloat16)
    grad_gate_out = (cotangent.astype(jnp.float32) * conv_seq).astype(jnp.bfloat16)
    factor = 1.0 / jnp.sqrt(jnp.float32(shared * SEQS * SEQ_LEN))
    grad_filters = (tap_total * factor).astype(jnp.float32)
    return (grad_values, grad_gate_in, grad_gate_out, grad_filters)
```

```python
import functools
import math

import jax
import jax.numpy as jnp
from jax import lax
from jax.experimental import pallas as pl
from jax.experimental.pallas import tpu as pltpu
from jax.sharding import PartitionSpec as P

HIGHEST = lax.Precision.HIGHEST


def as_sent(x):

    def short(part):
        return part.astype(jnp.bfloat16) if part.dtype == jnp.float32 else part

    return jax.tree.map(short, x)


def angle_table(first, second, period):
    left_idx = lax.broadcasted_iota(jnp.int32, (first, second), 0)
    right_idx = lax.broadcasted_iota(jnp.int32, (first, second), 1)
    angle = (left_idx * right_idx % period).astype(jnp.float32) * (2.0 * math.pi / period)
    return (jnp.cos(angle), jnp.sin(angle))


def dft_tables(used_rows, total_rows, columns):
    modulus = total_rows * columns
    cos_rows, sin_rows = angle_table(total_rows, used_rows, total_rows)
    k_twist = lax.broadcasted_iota(jnp.int32, (total_rows, 1, columns), 0)
    s_twist = lax.broadcasted_iota(jnp.int32, (total_rows, 1, columns), 2)
    angle_twist = (k_twist * s_twist % modulus).astype(jnp.float32) * (2.0 * math.pi / modulus)
    outer_len = max(
        [
            divisor
            for divisor in range(1, columns + 1)
            if columns % divisor == 0 and divisor * divisor <= columns
        ]
    )
    inner_len = columns // outer_len
    cos_outer, sin_outer = angle_table(outer_len, outer_len, outer_len)
    cos_inner, sin_inner = angle_table(inner_len, inner_len, inner_len)
    cos_small, sin_small = angle_table(outer_len, inner_len, columns)
    return (
        cos_rows,
        sin_rows,
        jnp.cos(angle_twist),
        jnp.sin(angle_twist),
        cos_outer,
        sin_outer,
        cos_inner,
        sin_inner,
        cos_small,
        sin_small,
        outer_len,
        inner_len,
        modulus,
    )


def by_rows(table, series):
    return jnp.einsum("kr,rcs->kcs", table, series, precision=HIGHEST)


def to_rows(table, series):
    return jnp.einsum("kr,kcs->rcs", table, series, precision=HIGHEST)


def by_outer(table, series):
    return jnp.einsum("ji,kcis->kcjs", table, series, precision=HIGHEST)


def by_inner(series, table):
    return jnp.einsum("kcjs,sq->kcjq", series, table, precision=HIGHEST)


def inner_forward(part_re, part_im, tables):
    cos_outer, sin_outer, cos_inner, sin_inner, cos_small, sin_small, outer_len, inner_len = tables[
        4:12
    ]
    shape = part_re.shape
    split_re = part_re.reshape(shape[0], shape[1], outer_len, inner_len)
    split_im = part_im.reshape(shape[0], shape[1], outer_len, inner_len)
    first_re = by_outer(cos_outer, split_re) + by_outer(sin_outer, split_im)
    first_im = by_outer(cos_outer, split_im) - by_outer(sin_outer, split_re)
    turned_re = first_re * cos_small + first_im * sin_small
    turned_im = first_im * cos_small - first_re * sin_small
    out_re = by_inner(turned_re, cos_inner) + by_inner(turned_im, sin_inner)
    out_im = by_inner(turned_im, cos_inner) - by_inner(turned_re, sin_inner)
    return (out_re.reshape(shape), out_im.reshape(shape))


def inner_inverse(part_re, part_im, tables):
    cos_outer, sin_outer, cos_inner, sin_inner, cos_small, sin_small, outer_len, inner_len = tables[
        4:12
    ]
    shape = part_re.shape
    split_re = part_re.reshape(shape[0], shape[1], outer_len, inner_len)
    split_im = part_im.reshape(shape[0], shape[1], outer_len, inner_len)
    first_re = by_inner(split_re, cos_inner) - by_inner(split_im, sin_inner)
    first_im = by_inner(split_im, cos_inner) + by_inner(split_re, sin_inner)
    turned_re = first_re * cos_small - first_im * sin_small
    turned_im = first_im * cos_small + first_re * sin_small
    out_re = by_outer(cos_outer, turned_re) - by_outer(sin_outer, turned_im)
    out_im = by_outer(cos_outer, turned_im) + by_outer(sin_outer, turned_re)
    return (out_re.reshape(shape), out_im.reshape(shape))


def spectrum(series, tables):
    cos_rows, sin_rows, cos_twist, sin_twist = tables[0:4]
    first_re = by_rows(cos_rows, series)
    first_im = -by_rows(sin_rows, series)
    turned_re = first_re * cos_twist + first_im * sin_twist
    turned_im = first_im * cos_twist - first_re * sin_twist
    return inner_forward(turned_re, turned_im, tables)


def synthesis(spec_re, spec_im, tables):
    cos_rows, sin_rows, cos_twist, sin_twist = tables[0:4]
    modulus = tables[12]
    inner_re, inner_im = inner_inverse(spec_re, spec_im, tables)
    turned_re = inner_re * cos_twist - inner_im * sin_twist
    turned_im = inner_im * cos_twist + inner_re * sin_twist
    result = to_rows(cos_rows, turned_re) - to_rows(sin_rows, turned_im)
    return result * (1.0 / modulus)


def to_owner(block):
    return jnp.swapaxes(block, 1, 2)[None]


def from_owner(block):
    return jnp.swapaxes(block[0], 1, 2)


def times_bf16(left, right):
    return (left.astype(jnp.float32) * right.astype(jnp.float32)).astype(jnp.bfloat16)


def spectral_body(values, gate_in, gate_out, cotangent, filters):
    seq_count = values.shape[0]
    tokens = values.shape[1]
    channels = values.shape[2]
    filter_count = filters.shape[0]
    shards = lax.axis_size("seq")
    replicas = lax.axis_size("batch")
    owned_count = channels // shards
    tables = dft_tables(shards, 2 * shards, tokens)

    def flatten_series(block):
        return block.reshape(block.shape[0], seq_count * owned_count, tokens)

    def grouped(block):
        return block.reshape(block.shape[0], seq_count, owned_count, tokens)

    spread = jnp.tile(filters, (channels // filter_count, 1)).reshape(1, channels, tokens)
    owned_taps = lax.all_to_all(spread, "seq", split_axis=1, concat_axis=0, tiled=True)
    tap_re, tap_im = spectrum(owned_taps, tables)
    tap_re = tap_re[:, None]
    tap_im = tap_im[:, None]
    mixed_in = times_bf16(values, gate_in)
    grad_mixed = times_bf16(cotangent, gate_out)
    owned_in, owned_grad = (
        lax.all_to_all(to_owner(mixed_in), "seq", split_axis=2, concat_axis=0, tiled=True),
        lax.all_to_all(to_owner(grad_mixed), "seq", split_axis=2, concat_axis=0, tiled=True),
    )
    in_re, in_im = spectrum(flatten_series(owned_in).astype(jnp.float32), tables)
    grad_re, grad_im = spectrum(flatten_series(owned_grad).astype(jnp.float32), tables)
    in_re = grouped(in_re)
    in_im = grouped(in_im)
    grad_re = grouped(grad_re)
    grad_im = grouped(grad_im)
    conv_out = grouped(
        synthesis(
            flatten_series(tap_re * in_re - tap_im * in_im),
            flatten_series(tap_re * in_im + tap_im * in_re),
            tables,
        )
    ).astype(jnp.bfloat16)
    grad_conv_in = grouped(
        synthesis(
            flatten_series(tap_re * grad_re + tap_im * grad_im),
            flatten_series(tap_re * grad_im - tap_im * grad_re),
            tables,
        )
    ).astype(jnp.bfloat16)
    tap_terms = synthesis(
        jnp.sum(in_re * grad_re + in_im * grad_im, axis=1),
        jnp.sum(in_re * grad_im - in_im * grad_re, axis=1),
        tables,
    )
    back_owned, conv_owned = (
        lax.all_to_all(grad_conv_in, "seq", split_axis=0, concat_axis=2, tiled=True),
        lax.all_to_all(conv_out, "seq", split_axis=0, concat_axis=2, tiled=True),
    )
    back_seq = from_owner(back_owned)
    conv_seq = from_owner(conv_owned)
    grad_values = times_bf16(gate_in, back_seq)
    grad_gate_in = times_bf16(values, back_seq)
    grad_gate_out = times_bf16(cotangent, conv_seq)
    tap_seq = lax.all_to_all(
        as_sent(tap_terms), "seq", split_axis=0, concat_axis=1, tiled=True
    ).astype(tap_terms.dtype)
    shared = channels * replicas // filter_count
    factor = 1.0 / math.sqrt(shared * seq_count * shards * tokens)
    per_filter = (
        tap_seq.reshape(channels // filter_count, filter_count, tokens).sum(axis=0) * factor
    )
    grad_filters = lax.psum_scatter(
        per_filter.astype(jnp.bfloat16), "batch", scatter_dimension=0, tiled=True
    ).astype(jnp.float32)
    return (grad_values, grad_gate_in, grad_gate_out, grad_filters)


LANES = 128
MESH = pl.DeviceIdType.MESH


def kernel(
    dims,
    values_ref,
    gate_in_ref,
    gate_out_ref,
    cotangent_ref,
    filters_ref,
    grad_values_ref,
    grad_gate_in_ref,
    grad_gate_out_ref,
    grad_filters_ref,
    sent,
    held,
    held_taps,
    taps_rows,
    series,
    padded,
    result,
    result_sent,
    result_held,
    tap_rows,
    tap_sent,
    tap_held,
    own_sem,
    in_send,
    in_recv,
    taps_send,
    taps_recv,
    out_send,
    out_recv,
    term_send,
    term_recv,
):
    shards, replicas, tokens, own, reps, factor = dims
    halves = tokens // LANES
    blocks = shards * halves
    lines = 2 * reps * own
    group = own * shards
    me = lax.axis_index("seq")
    row = lax.axis_index("batch")
    flat = me * replicas + row
    f32, bf16 = jnp.float32, jnp.bfloat16

    barrier = pltpu.get_barrier_semaphore()
    for step in range(1, shards * replicas):
        other = lax.rem(flat + step, shards * replicas)
        pl.semaphore_signal(
            barrier,
            inc=1,
            device_id={"seq": other // replicas, "batch": lax.rem(other, replicas)},
            device_id_type=MESH,
        )

    down = lax.broadcasted_iota(jnp.int32, (LANES, LANES), 0)
    across = lax.broadcasted_iota(jnp.int32, (LANES, LANES), 1)
    later = across >= down
    mirror = jnp.where(down + across == LANES - 1, 1.0, 0.0).astype(bf16)

    def product(left, right):
        return (left.astype(f32) * right.astype(f32)).astype(bf16)

    for half in range(halves):
        rows = pl.ds(half * LANES, LANES)
        mixed = product(values_ref[0, rows, :], gate_in_ref[0, rows, :])
        grad = product(cotangent_ref[0, rows, :], gate_out_ref[0, rows, :])
        mixed_t = mixed.astype(f32).T
        grad_t = jnp.dot(mirror, grad, preferred_element_type=f32).T
        for owner in range(shards):
            parts = [
                part[rep * group + owner * own : rep * group + (owner + 1) * own]
                for part in (mixed_t, grad_t)
                for rep in range(reps)
            ]
            sent[owner, half * lines : (half + 1) * lines, :] = jnp.concatenate(parts, 0).astype(bf16)

    pl.semaphore_wait(barrier, shards * replicas - 1)

    def taps_copy(source_owner, slot, peer):
        return pltpu.make_async_remote_copy(
            src_ref=filters_ref.at[pl.ds(pl.multiple_of(source_owner * own, own), own), :],
            dst_ref=held_taps.at[slot],
            send_sem=taps_send.at[peer],
            recv_sem=taps_recv.at[slot],
            device_id={"seq": peer},
            device_id_type=MESH,
        )

    def in_copy(source_owner, slot, peer):
        return pltpu.make_async_remote_copy(
            src_ref=sent.at[source_owner],
            dst_ref=held.at[slot],
            send_sem=in_send.at[peer],
            recv_sem=in_recv.at[slot],
            device_id={"seq": peer},
            device_id_type=MESH,
        )

    def out_copy(slot, peer):
        return pltpu.make_async_remote_copy(
            src_ref=result_sent.at[peer],
            dst_ref=result_held.at[slot],
            send_sem=out_send.at[peer],
            recv_sem=out_recv.at[slot],
            device_id={"seq": peer},
            device_id_type=MESH,
        )

    peers = [lax.rem(me + step, shards) for step in range(1, shards)]
    for peer in peers:
        taps_copy(peer, me, peer).start()
        in_copy(peer, me, peer).start()
    own_taps = pltpu.make_async_copy(
        filters_ref.at[pl.ds(pl.multiple_of(me * own, own), own), :], held_taps.at[me], own_sem.at[0]
    )
    own_in = pltpu.make_async_copy(sent.at[me], held.at[me], own_sem.at[1])
    own_taps.start()
    own_in.start()
    zero_rows = jnp.zeros((blocks, LANES), f32)
    for rep in range(reps):
        padded[rep, 0:blocks, :] = zero_rows
        padded[reps + rep, blocks : 2 * blocks, :] = zero_rows
    own_taps.wait()
    own_in.wait()
    for peer in peers:
        taps_copy(peer, peer, peer).wait_recv()
        in_copy(peer, peer, peer).wait_recv()
    for source in range(shards):
        series[source * halves * lines : (source + 1) * halves * lines, :] = held[source].astype(f32)
        for half in range(halves):
            k = source * halves + half
            taps_rows[k * own : (k + 1) * own, :] = held_taps[
                source, :, half * LANES : (half + 1) * LANES
            ]

    def one_filter(f, carry):
        for line in range(2 * reps):
            at = 0 if line >= reps else blocks
            padded[line, at : at + blocks, :] = series[pl.ds(line * own + f, blocks, stride=lines), :]
        grad_cols = jnp.concatenate(
            [padded[reps + rep, 0:blocks, :] for rep in range(reps)], 0
        ).T.astype(bf16)
        total = jnp.zeros((2 * reps * blocks, LANES), f32)
        turned_before = jnp.zeros((LANES, LANES), f32)
        gram_before = None
        for pair in range(blocks // 2):
            lefts, rights = [], []
            for k in (2 * pair, 2 * pair + 1):
                taps = jnp.tile(taps_rows[pl.ds(k * own + f, 8, stride=0), :], (LANES // 8, 1))
                turned = pltpu.roll(taps, 0, 1, stride=1, stride_axis=0)
                rights.append(jnp.where(later, turned, turned_before).astype(bf16))
                turned_before = turned
                lefts.append(
                    jnp.concatenate(
                        [padded[rep, blocks - k : 2 * blocks - k, :] for rep in range(reps)]
                        + [padded[reps + rep, k : blocks + k, :] for rep in range(reps)],
                        0,
                    ).astype(bf16)
                )
            left = jnp.concatenate(lefts, 1)
            total = total + jnp.dot(left, jnp.concatenate(rights, 0), preferred_element_type=f32)
            gram = jnp.dot(grad_cols, left[: reps * blocks], preferred_element_type=f32)
            for at in range(2):
                k = 2 * pair + at
                gram_now = pltpu.roll(
                    gram[:, at * LANES : (at + 1) * LANES], 0, 1, stride=1, stride_axis=0
                )
                if k > 0:
                    tap_rows[pl.ds((k - 1) * own + f, 1), :] = jnp.sum(
                        jnp.where(later, gram_before, gram_now), axis=0, keepdims=True
                    )
                gram_before = gram_now
        tap_rows[pl.ds((blocks - 1) * own + f, 1), :] = jnp.sum(
            jnp.where(later, gram_before, 0.0), axis=0, keepdims=True
        )
        for line in range(2 * reps):
            result[pl.ds(line * own + f, blocks, stride=lines), :] = total[
                line * blocks : (line + 1) * blocks
            ]
        return carry

    lax.fori_loop(0, own, one_filter, 0)

    for peer in range(shards):
        result_sent[peer] = result[
            peer * halves * lines : (peer + 1) * halves * lines, :
        ].astype(bf16)
    terms = jnp.dot(tap_rows[...].astype(bf16), mirror, preferred_element_type=f32).astype(bf16)
    for peer in range(shards):
        tap_sent[peer] = terms[peer * halves * own : (peer + 1) * halves * own]

    for peer in peers:
        out_copy(me, peer).start()
    own_out = pltpu.make_async_copy(result_sent.at[me], result_held.at[me], own_sem.at[0])
    own_out.start()

    per_row = shards // replicas
    goal = me // per_row
    slot_here = lax.rem(me, per_row) * replicas + row

    def term_copy(peer, to_row, slot):
        return pltpu.make_async_remote_copy(
            src_ref=tap_sent.at[peer],
            dst_ref=tap_held.at[slot],
            send_sem=term_send.at[peer],
            recv_sem=term_recv.at[slot],
            device_id={"seq": peer, "batch": to_row},
            device_id_type=MESH,
        )

    own_term = pltpu.make_async_copy(tap_sent.at[me], tap_held.at[slot_here], own_sem.at[1])
    stays = goal == row
    for peer in peers:
        term_copy(peer, goal, slot_here).start()

    @pl.when(stays)
    def _():
        own_term.start()

    @pl.when(jnp.logical_not(stays))
    def _():
        term_copy(me, goal, slot_here).start()

    own_out.wait()
    for peer in peers:
        out_copy(peer, peer).wait_recv()

    for half in range(halves):
        rows = pl.ds(half * LANES, LANES)
        moved = []
        for kind in range(2):
            at = half * lines + kind * reps * own
            block = jnp.concatenate(
                [
                    result_held[source, at + rep * own : at + (rep + 1) * own, :].astype(f32)
                    for rep in range(reps)
                    for source in range(shards)
                ],
                0,
            )
            moved.append(block.T)
        conv = moved[0]
        back = jnp.dot(mirror, moved[1].astype(bf16), preferred_element_type=f32)
        grad_values_ref[0, rows, :] = (gate_in_ref[0, rows, :].astype(f32) * back).astype(bf16)
        grad_gate_in_ref[0, rows, :] = (values_ref[0, rows, :].astype(f32) * back).astype(bf16)
        grad_gate_out_ref[0, rows, :] = (cotangent_ref[0, rows, :].astype(f32) * conv).astype(bf16)

    for at in range(per_row):
        for source_row in range(replicas):
            slot = at * replicas + source_row
            local = jnp.logical_and(me == row * per_row + at, row == source_row)

            @pl.when(local)
            def _():
                own_term.wait()

            @pl.when(jnp.logical_not(local))
            def _(slot=slot):
                term_copy(me, row, slot).wait_recv()

    for at in range(per_row):
        summed = sum(
            tap_held[at * replicas + source_row].astype(f32) for source_row in range(replicas)
        )
        for half in range(halves):
            grad_filters_ref[at * own : (at + 1) * own, half * LANES : (half + 1) * LANES] = (
                summed[half * own : (half + 1) * own] * factor
            )

    for peer in peers:
        taps_copy(peer, me, peer).wait_send()
        in_copy(peer, me, peer).wait_send()
        out_copy(me, peer).wait_send()
        term_copy(peer, goal, slot_here).wait_send()

    @pl.when(jnp.logical_not(stays))
    def _():
        term_copy(me, goal, slot_here).wait_send()


def direct_body(values, gate_in, gate_out, cotangent, filters):
    tokens, channels = values.shape[1:]
    filter_count = filters.shape[0]
    shards = lax.axis_size("seq")
    replicas = lax.axis_size("batch")
    own = filter_count // shards
    reps = channels // filter_count
    halves = tokens // LANES
    blocks = shards * halves
    lines = 2 * reps * own
    factor = 1.0 / math.sqrt(reps * replicas * shards * tokens)
    vmem = pl.BlockSpec(memory_space=pltpu.VMEM)
    f32, bf16 = jnp.float32, jnp.bfloat16
    slab = jax.ShapeDtypeStruct(values.shape, bf16)
    sems = pltpu.SemaphoreType.DMA((shards,))
    return pl.pallas_call(
        functools.partial(kernel, (shards, replicas, tokens, own, reps, factor)),
        out_shape=(
            slab,
            slab,
            slab,
            jax.ShapeDtypeStruct((filter_count // replicas, tokens), f32),
        ),
        in_specs=[vmem] * 5,
        out_specs=(vmem,) * 4,
        scratch_shapes=[
            pltpu.VMEM((shards, halves * lines, LANES), bf16),
            pltpu.VMEM((shards, halves * lines, LANES), bf16),
            pltpu.VMEM((shards, own, tokens), f32),
            pltpu.VMEM((blocks * own + 8, LANES), f32),
            pltpu.VMEM((blocks * lines, LANES), f32),
            pltpu.VMEM((2 * reps, 2 * blocks, LANES), f32),
            pltpu.VMEM((blocks * lines, LANES), f32),
            pltpu.VMEM((shards, halves * lines, LANES), bf16),
            pltpu.VMEM((shards, halves * lines, LANES), bf16),
            pltpu.VMEM((blocks * own, LANES), f32),
            pltpu.VMEM((shards, halves * own, LANES), bf16),
            pltpu.VMEM((shards, halves * own, LANES), bf16),
            pltpu.SemaphoreType.DMA((2,)),
        ]
        + [sems] * 8,
        compiler_params=pltpu.CompilerParams(collective_id=0, has_side_effects=True),
    )(values, gate_in, gate_out, cotangent, filters)


def body(values, gate_in, gate_out, cotangent, filters):
    seqs, tokens, channels = values.shape
    filter_count = filters.shape[0]
    shards = lax.axis_size("seq")
    replicas = lax.axis_size("batch")
    direct = (
        seqs == 1
        and channels == LANES
        and tokens % LANES == 0
        and channels % filter_count == 0
        and filter_count % (8 * shards) == 0
        and shards % replicas == 0
    )
    chosen = direct_body if direct else spectral_body
    return chosen(values, gate_in, gate_out, cotangent, filters)


def solution(mesh):
    placed = (
        P(None, "seq", "batch"),
        P(None, "seq", "batch"),
        P(None, "seq", "batch"),
        P(None, "seq", "batch"),
        P(None, "seq"),
    )
    return jax.shard_map(
        body,
        mesh=mesh,
        in_specs=placed,
        out_specs=(
            P(None, "seq", "batch"),
            P(None, "seq", "batch"),
            P(None, "seq", "batch"),
            P("batch", "seq"),
        ),
        check_vma=False,
    )
```

```python
import functools
import math

import jax
import jax.numpy as jnp
from jax import lax
from jax.experimental import pallas as pl
from jax.experimental.pallas import tpu as pltpu
from jax.sharding import PartitionSpec as P

HIGHEST = lax.Precision.HIGHEST


def as_sent(x):

    def short(part):
        return part.astype(jnp.bfloat16) if part.dtype == jnp.float32 else part

    return jax.tree.map(short, x)


def angle_table(first, second, period):
    left_idx = lax.broadcasted_iota(jnp.int32, (first, second), 0)
    right_idx = lax.broadcasted_iota(jnp.int32, (first, second), 1)
    angle = (left_idx * right_idx % period).astype(jnp.float32) * (2.0 * math.pi / period)
    return (jnp.cos(angle), jnp.sin(angle))


def dft_tables(used_rows, total_rows, columns):
    modulus = total_rows * columns
    cos_rows, sin_rows = angle_table(total_rows, used_rows, total_rows)
    k_twist = lax.broadcasted_iota(jnp.int32, (total_rows, 1, columns), 0)
    s_twist = lax.broadcasted_iota(jnp.int32, (total_rows, 1, columns), 2)
    angle_twist = (k_twist * s_twist % modulus).astype(jnp.float32) * (2.0 * math.pi / modulus)
    outer_len = max(
        [
            divisor
            for divisor in range(1, columns + 1)
            if columns % divisor == 0 and divisor * divisor <= columns
        ]
    )
    inner_len = columns // outer_len
    cos_outer, sin_outer = angle_table(outer_len, outer_len, outer_len)
    cos_inner, sin_inner = angle_table(inner_len, inner_len, inner_len)
    cos_small, sin_small = angle_table(outer_len, inner_len, columns)
    return (
        cos_rows,
        sin_rows,
        jnp.cos(angle_twist),
        jnp.sin(angle_twist),
        cos_outer,
        sin_outer,
        cos_inner,
        sin_inner,
        cos_small,
        sin_small,
        outer_len,
        inner_len,
        modulus,
    )


def by_rows(table, series):
    return jnp.einsum("kr,rcs->kcs", table, series, precision=HIGHEST)


def to_rows(table, series):
    return jnp.einsum("kr,kcs->rcs", table, series, precision=HIGHEST)


def by_outer(table, series):
    return jnp.einsum("ji,kcis->kcjs", table, series, precision=HIGHEST)


def by_inner(series, table):
    return jnp.einsum("kcjs,sq->kcjq", series, table, precision=HIGHEST)


def inner_forward(part_re, part_im, tables):
    cos_outer, sin_outer, cos_inner, sin_inner, cos_small, sin_small, outer_len, inner_len = tables[
        4:12
    ]
    shape = part_re.shape
    split_re = part_re.reshape(shape[0], shape[1], outer_len, inner_len)
    split_im = part_im.reshape(shape[0], shape[1], outer_len, inner_len)
    first_re = by_outer(cos_outer, split_re) + by_outer(sin_outer, split_im)
    first_im = by_outer(cos_outer, split_im) - by_outer(sin_outer, split_re)
    turned_re = first_re * cos_small + first_im * sin_small
    turned_im = first_im * cos_small - first_re * sin_small
    out_re = by_inner(turned_re, cos_inner) + by_inner(turned_im, sin_inner)
    out_im = by_inner(turned_im, cos_inner) - by_inner(turned_re, sin_inner)
    return (out_re.reshape(shape), out_im.reshape(shape))


def inner_inverse(part_re, part_im, tables):
    cos_outer, sin_outer, cos_inner, sin_inner, cos_small, sin_small, outer_len, inner_len = tables[
        4:12
    ]
    shape = part_re.shape
    split_re = part_re.reshape(shape[0], shape[1], outer_len, inner_len)
    split_im = part_im.reshape(shape[0], shape[1], outer_len, inner_len)
    first_re = by_inner(split_re, cos_inner) - by_inner(split_im, sin_inner)
    first_im = by_inner(split_im, cos_inner) + by_inner(split_re, sin_inner)
    turned_re = first_re * cos_small - first_im * sin_small
    turned_im = first_im * cos_small + first_re * sin_small
    out_re = by_outer(cos_outer, turned_re) - by_outer(sin_outer, turned_im)
    out_im = by_outer(cos_outer, turned_im) + by_outer(sin_outer, turned_re)
    return (out_re.reshape(shape), out_im.reshape(shape))


def spectrum(series, tables):
    cos_rows, sin_rows, cos_twist, sin_twist = tables[0:4]
    first_re = by_rows(cos_rows, series)
    first_im = -by_rows(sin_rows, series)
    turned_re = first_re * cos_twist + first_im * sin_twist
    turned_im = first_im * cos_twist - first_re * sin_twist
    return inner_forward(turned_re, turned_im, tables)


def synthesis(spec_re, spec_im, tables):
    cos_rows, sin_rows, cos_twist, sin_twist = tables[0:4]
    modulus = tables[12]
    inner_re, inner_im = inner_inverse(spec_re, spec_im, tables)
    turned_re = inner_re * cos_twist - inner_im * sin_twist
    turned_im = inner_im * cos_twist + inner_re * sin_twist
    result = to_rows(cos_rows, turned_re) - to_rows(sin_rows, turned_im)
    return result * (1.0 / modulus)


def to_owner(block):
    return jnp.swapaxes(block, 1, 2)[None]


def from_owner(block):
    return jnp.swapaxes(block[0], 1, 2)


def times_bf16(left, right):
    return (left.astype(jnp.float32) * right.astype(jnp.float32)).astype(jnp.bfloat16)


def spectral_body(values, gate_in, gate_out, cotangent, filters):
    seq_count = values.shape[0]
    tokens = values.shape[1]
    channels = values.shape[2]
    filter_count = filters.shape[0]
    shards = lax.axis_size("seq")
    replicas = lax.axis_size("batch")
    owned_count = channels // shards
    tables = dft_tables(shards, 2 * shards, tokens)

    def flatten_series(block):
        return block.reshape(block.shape[0], seq_count * owned_count, tokens)

    def grouped(block):
        return block.reshape(block.shape[0], seq_count, owned_count, tokens)

    spread = jnp.tile(filters, (channels // filter_count, 1)).reshape(1, channels, tokens)
    owned_taps = lax.all_to_all(spread, "seq", split_axis=1, concat_axis=0, tiled=True)
    tap_re, tap_im = spectrum(owned_taps, tables)
    tap_re = tap_re[:, None]
    tap_im = tap_im[:, None]
    mixed_in = times_bf16(values, gate_in)
    grad_mixed = times_bf16(cotangent, gate_out)
    owned_in, owned_grad = (
        lax.all_to_all(to_owner(mixed_in), "seq", split_axis=2, concat_axis=0, tiled=True),
        lax.all_to_all(to_owner(grad_mixed), "seq", split_axis=2, concat_axis=0, tiled=True),
    )
    in_re, in_im = spectrum(flatten_series(owned_in).astype(jnp.float32), tables)
    grad_re, grad_im = spectrum(flatten_series(owned_grad).astype(jnp.float32), tables)
    in_re = grouped(in_re)
    in_im = grouped(in_im)
    grad_re = grouped(grad_re)
    grad_im = grouped(grad_im)
    conv_out = grouped(
        synthesis(
            flatten_series(tap_re * in_re - tap_im * in_im),
            flatten_series(tap_re * in_im + tap_im * in_re),
            tables,
        )
    ).astype(jnp.bfloat16)
    grad_conv_in = grouped(
        synthesis(
            flatten_series(tap_re * grad_re + tap_im * grad_im),
            flatten_series(tap_re * grad_im - tap_im * grad_re),
            tables,
        )
    ).astype(jnp.bfloat16)
    tap_terms = synthesis(
        jnp.sum(in_re * grad_re + in_im * grad_im, axis=1),
        jnp.sum(in_re * grad_im - in_im * grad_re, axis=1),
        tables,
    )
    back_owned, conv_owned = (
        lax.all_to_all(grad_conv_in, "seq", split_axis=0, concat_axis=2, tiled=True),
        lax.all_to_all(conv_out, "seq", split_axis=0, concat_axis=2, tiled=True),
    )
    back_seq = from_owner(back_owned)
    conv_seq = from_owner(conv_owned)
    grad_values = times_bf16(gate_in, back_seq)
    grad_gate_in = times_bf16(values, back_seq)
    grad_gate_out = times_bf16(cotangent, conv_seq)
    tap_seq = lax.all_to_all(
        as_sent(tap_terms), "seq", split_axis=0, concat_axis=1, tiled=True
    ).astype(tap_terms.dtype)
    shared = channels * replicas // filter_count
    factor = 1.0 / math.sqrt(shared * seq_count * shards * tokens)
    per_filter = (
        tap_seq.reshape(channels // filter_count, filter_count, tokens).sum(axis=0) * factor
    )
    grad_filters = lax.psum_scatter(
        per_filter.astype(jnp.bfloat16), "batch", scatter_dimension=0, tiled=True
    ).astype(jnp.float32)
    return (grad_values, grad_gate_in, grad_gate_out, grad_filters)


LANES = 128
MESH = pl.DeviceIdType.MESH


def kernel(
    dims,
    values_ref,
    gate_in_ref,
    gate_out_ref,
    cotangent_ref,
    filters_ref,
    result_held,
    tap_held,
    values_here,
    gate_in_here,
    gate_out_here,
    cotangent_here,
    sent,
    held,
    held_taps,
    taps_rows,
    series,
    padded,
    result,
    result_sent,
    tap_rows,
    tap_sent,
    own_sem,
    in_send,
    in_recv,
    taps_send,
    taps_recv,
    out_send,
    out_recv,
    term_send,
    term_recv,
    load_sem,
    near,
):
    shards, replicas, tokens, own, reps, factor = dims
    halves = tokens // LANES
    blocks = shards * halves
    lines = 2 * reps * own
    group = own * shards
    me = lax.axis_index("seq")
    row = lax.axis_index("batch")
    f32, bf16 = jnp.float32, jnp.bfloat16

    barrier = pltpu.get_barrier_semaphore()
    peers = [lax.rem(me + step, shards) for step in range(1, shards)]
    for peer in peers:
        pl.semaphore_signal(barrier, inc=1, device_id={"seq": peer}, device_id_type=MESH)
    has_below = row > 0
    has_above = row < replicas - 1
    neighbours = has_below.astype(jnp.int32) + has_above.astype(jnp.int32)

    def greet(semaphore):
        @pl.when(has_below)
        def _():
            pl.semaphore_signal(semaphore, inc=1, device_id={"batch": row - 1}, device_id_type=MESH)

        @pl.when(has_above)
        def _():
            pl.semaphore_signal(semaphore, inc=1, device_id={"batch": row + 1}, device_id_type=MESH)

    greet(barrier)
    loads = [
        pltpu.make_async_copy(source, here, load_sem.at[at])
        for at, (source, here) in enumerate(
            (
                (values_ref, values_here),
                (gate_in_ref, gate_in_here),
                (cotangent_ref, cotangent_here),
                (gate_out_ref, gate_out_here),
            )
        )
    ]
    for load in loads:
        load.start()

    down = lax.broadcasted_iota(jnp.int32, (LANES, LANES), 0)
    across = lax.broadcasted_iota(jnp.int32, (LANES, LANES), 1)
    later = across >= down
    mirror = jnp.where(down + across == LANES - 1, 1.0, 0.0).astype(bf16)

    def product(left, right):
        return (left.astype(f32) * right.astype(f32)).astype(bf16)

    for load in loads:
        load.wait()
    for half in range(halves):
        rows = pl.ds(half * LANES, LANES)
        mixed = product(values_here[0, rows, :], gate_in_here[0, rows, :])
        grad = product(cotangent_here[0, rows, :], gate_out_here[0, rows, :])
        mixed_t = mixed.astype(f32).T
        grad_t = jnp.dot(mirror, grad, preferred_element_type=f32).T
        for owner in range(shards):
            parts = [
                part[rep * group + owner * own : rep * group + (owner + 1) * own]
                for part in (mixed_t, grad_t)
                for rep in range(reps)
            ]
            sent[owner, half * lines : (half + 1) * lines, :] = jnp.concatenate(parts, 0).astype(bf16)

    pl.semaphore_wait(barrier, shards - 1 + neighbours)
    if replicas > 1:
        greet(near.at[0])

    def taps_copy(source_owner, slot, peer):
        return pltpu.make_async_remote_copy(
            src_ref=filters_ref.at[pl.ds(pl.multiple_of(source_owner * own, own), own), :],
            dst_ref=held_taps.at[slot],
            send_sem=taps_send.at[peer],
            recv_sem=taps_recv.at[slot],
            device_id={"seq": peer},
            device_id_type=MESH,
        )

    def in_copy(source_owner, slot, peer):
        return pltpu.make_async_remote_copy(
            src_ref=sent.at[source_owner],
            dst_ref=held.at[slot],
            send_sem=in_send.at[peer],
            recv_sem=in_recv.at[slot],
            device_id={"seq": peer},
            device_id_type=MESH,
        )

    def out_copy(slot, peer):
        return pltpu.make_async_remote_copy(
            src_ref=result_sent.at[peer],
            dst_ref=result_held.at[slot],
            send_sem=out_send.at[peer],
            recv_sem=out_recv.at[slot],
            device_id={"seq": peer},
            device_id_type=MESH,
        )

    for peer in peers:
        in_copy(peer, me, peer).start()
    own_in = pltpu.make_async_copy(sent.at[me], held.at[me], own_sem.at[0])
    own_in.start()
    for peer in peers:
        taps_copy(peer, me, peer).start()
    own_taps = pltpu.make_async_copy(
        filters_ref.at[pl.ds(pl.multiple_of(me * own, own), own), :], held_taps.at[me], own_sem.at[1]
    )
    own_taps.start()
    zero_rows = jnp.zeros((blocks, LANES), f32)
    for rep in range(reps):
        padded[rep, 0:blocks, :] = zero_rows
        padded[reps + rep, blocks : 2 * blocks, :] = zero_rows
    for hop in range(1, replicas - 1):
        pl.semaphore_wait(near.at[hop - 1], neighbours)
        greet(near.at[hop])
    own_in.wait()
    for peer in peers:
        in_copy(peer, peer, peer).wait_recv()
    for source in range(shards):
        series[source * halves * lines : (source + 1) * halves * lines, :] = held[source].astype(f32)

    def place(f):
        for line in range(2 * reps):
            at = 0 if line >= reps else blocks
            padded[line, at : at + blocks, :] = series[pl.ds(line * own + f, blocks, stride=lines), :]

    def one_gram(f, carry):
        place(f)
        grad_cols = jnp.concatenate(
            [padded[reps + rep, 0:blocks, :] for rep in range(reps)], 0
        ).T.astype(bf16)
        gram_before = None
        for pair in range(blocks // 2):
            left = jnp.concatenate(
                [
                    jnp.concatenate(
                        [padded[rep, blocks - k : 2 * blocks - k, :] for rep in range(reps)], 0
                    ).astype(bf16)
                    for k in (2 * pair, 2 * pair + 1)
                ],
                1,
            )
            gram = jnp.dot(grad_cols, left, preferred_element_type=f32)
            for at in range(2):
                k = 2 * pair + at
                gram_now = pltpu.roll(
                    gram[:, at * LANES : (at + 1) * LANES], 0, 1, stride=1, stride_axis=0
                )
                if k > 0:
                    tap_rows[pl.ds((k - 1) * own + f, 1), :] = jnp.sum(
                        jnp.where(later, gram_before, gram_now), axis=0, keepdims=True
                    )
                gram_before = gram_now
        tap_rows[pl.ds((blocks - 1) * own + f, 1), :] = jnp.sum(
            jnp.where(later, gram_before, 0.0), axis=0, keepdims=True
        )
        return carry

    lax.fori_loop(0, own, one_gram, 0)

    terms = jnp.dot(tap_rows[...].astype(bf16), mirror, preferred_element_type=f32).astype(bf16)
    for peer in range(shards):
        tap_sent[peer] = terms[peer * halves * own : (peer + 1) * halves * own]

    per_row = shards // replicas
    goal = me // per_row
    slot_here = lax.rem(me, per_row) * replicas + row

    def term_copy(peer, to_row, slot):
        return pltpu.make_async_remote_copy(
            src_ref=tap_sent.at[peer],
            dst_ref=tap_held.at[slot],
            send_sem=term_send.at[peer],
            recv_sem=term_recv.at[slot],
            device_id={"seq": peer, "batch": to_row},
            device_id_type=MESH,
        )

    own_term = pltpu.make_async_copy(tap_sent.at[me], tap_held.at[slot_here], own_sem.at[2])
    stays = goal == row
    if replicas > 1:
        pl.semaphore_wait(near.at[replicas - 2], neighbours)
    for peer in peers:
        term_copy(peer, goal, slot_here).start()

    @pl.when(stays)
    def _():
        own_term.start()

    @pl.when(jnp.logical_not(stays))
    def _():
        term_copy(me, goal, slot_here).start()

    own_taps.wait()
    for peer in peers:
        taps_copy(peer, peer, peer).wait_recv()
    for source in range(shards):
        for half in range(halves):
            k = source * halves + half
            taps_rows[k * own : (k + 1) * own, :] = held_taps[
                source, :, half * LANES : (half + 1) * LANES
            ]

    def one_filter(f, carry):
        place(f)
        total = jnp.zeros((2 * reps * blocks, LANES), f32)
        turned_before = jnp.zeros((LANES, LANES), f32)
        for pair in range(blocks // 2):
            lefts, rights = [], []
            for k in (2 * pair, 2 * pair + 1):
                taps = jnp.tile(taps_rows[pl.ds(k * own + f, 8, stride=0), :], (LANES // 8, 1))
                turned = pltpu.roll(taps, 0, 1, stride=1, stride_axis=0)
                rights.append(jnp.where(later, turned, turned_before).astype(bf16))
                turned_before = turned
                lefts.append(
                    jnp.concatenate(
                        [padded[rep, blocks - k : 2 * blocks - k, :] for rep in range(reps)]
                        + [padded[reps + rep, k : blocks + k, :] for rep in range(reps)],
                        0,
                    ).astype(bf16)
                )
            total = total + jnp.dot(
                jnp.concatenate(lefts, 1),
                jnp.concatenate(rights, 0),
                preferred_element_type=f32,
            )
        for line in range(2 * reps):
            result[pl.ds(line * own + f, blocks, stride=lines), :] = total[
                line * blocks : (line + 1) * blocks
            ]
        return carry

    lax.fori_loop(0, own, one_filter, 0)

    for peer in range(shards):
        result_sent[peer] = result[
            peer * halves * lines : (peer + 1) * halves * lines, :
        ].astype(bf16)
    for peer in peers:
        out_copy(me, peer).start()
    own_out = pltpu.make_async_copy(result_sent.at[me], result_held.at[me], own_sem.at[0])
    own_out.start()
    own_out.wait()
    for peer in peers:
        out_copy(peer, peer).wait_recv()

    for at in range(per_row):
        for source_row in range(replicas):
            slot = at * replicas + source_row
            local = jnp.logical_and(me == row * per_row + at, row == source_row)

            @pl.when(local)
            def _():
                own_term.wait()

            @pl.when(jnp.logical_not(local))
            def _(slot=slot):
                term_copy(me, row, slot).wait_recv()

    for peer in peers:
        taps_copy(peer, me, peer).wait_send()
        in_copy(peer, me, peer).wait_send()
        out_copy(me, peer).wait_send()
        term_copy(peer, goal, slot_here).wait_send()

    @pl.when(jnp.logical_not(stays))
    def _():
        term_copy(me, goal, slot_here).wait_send()


def finish(
    dims,
    values_ref,
    gate_in_ref,
    cotangent_ref,
    result_held,
    tap_held,
    grad_values_ref,
    grad_gate_in_ref,
    grad_gate_out_ref,
    grad_filters_ref,
):
    shards, replicas, tokens, own, reps, factor = dims
    halves = tokens // LANES
    lines = 2 * reps * own
    f32, bf16 = jnp.float32, jnp.bfloat16
    down = lax.broadcasted_iota(jnp.int32, (LANES, LANES), 0)
    across = lax.broadcasted_iota(jnp.int32, (LANES, LANES), 1)
    mirror = jnp.where(down + across == LANES - 1, 1.0, 0.0).astype(bf16)
    for half in range(halves):
        rows = pl.ds(half * LANES, LANES)
        moved = []
        for kind in range(2):
            at = half * lines + kind * reps * own
            block = jnp.concatenate(
                [
                    result_held[source, at + rep * own : at + (rep + 1) * own, :].astype(f32)
                    for rep in range(reps)
                    for source in range(shards)
                ],
                0,
            )
            moved.append(block.T)
        conv = moved[0]
        back = jnp.dot(mirror, moved[1].astype(bf16), preferred_element_type=f32)
        grad_values_ref[0, rows, :] = (gate_in_ref[0, rows, :].astype(f32) * back).astype(bf16)
        grad_gate_in_ref[0, rows, :] = (values_ref[0, rows, :].astype(f32) * back).astype(bf16)
        grad_gate_out_ref[0, rows, :] = (cotangent_ref[0, rows, :].astype(f32) * conv).astype(bf16)
    for at in range(shards // replicas):
        summed = sum(
            tap_held[at * replicas + source_row].astype(f32) for source_row in range(replicas)
        )
        for half in range(halves):
            grad_filters_ref[at * own : (at + 1) * own, half * LANES : (half + 1) * LANES] = (
                summed[half * own : (half + 1) * own] * factor
            )


def direct_body(values, gate_in, gate_out, cotangent, filters):
    tokens, channels = values.shape[1:]
    filter_count = filters.shape[0]
    shards = lax.axis_size("seq")
    replicas = lax.axis_size("batch")
    own = filter_count // shards
    reps = channels // filter_count
    halves = tokens // LANES
    blocks = shards * halves
    lines = 2 * reps * own
    factor = 1.0 / math.sqrt(reps * replicas * shards * tokens)
    vmem = pl.BlockSpec(memory_space=pltpu.VMEM)
    anywhere = pl.BlockSpec(memory_space=pl.ANY)
    f32, bf16 = jnp.float32, jnp.bfloat16
    slab = jax.ShapeDtypeStruct(values.shape, bf16)
    sems = pltpu.SemaphoreType.DMA((shards,))
    dims = (shards, replicas, tokens, own, reps, factor)
    message = (shards, halves * lines, LANES)
    results, terms = pl.pallas_call(
        functools.partial(kernel, dims),
        out_shape=(
            jax.ShapeDtypeStruct(message, bf16),
            jax.ShapeDtypeStruct((shards, halves * own, LANES), bf16),
        ),
        in_specs=[anywhere] * 5,
        out_specs=(anywhere,) * 2,
        scratch_shapes=[pltpu.VMEM(values.shape, bf16)] * 4
        + [
            pltpu.VMEM(message, bf16),
            pltpu.VMEM(message, bf16),
            pltpu.VMEM((shards, own, tokens), f32),
            pltpu.VMEM((blocks * own + 8, LANES), f32),
            pltpu.VMEM((blocks * lines, LANES), f32),
            pltpu.VMEM((2 * reps, 2 * blocks, LANES), f32),
            pltpu.VMEM((blocks * lines, LANES), f32),
            pltpu.VMEM(message, bf16),
            pltpu.VMEM((blocks * own, LANES), f32),
            pltpu.VMEM((shards, halves * own, LANES), bf16),
            pltpu.SemaphoreType.DMA((3,)),
        ]
        + [sems] * 8
        + [pltpu.SemaphoreType.DMA((4,)), pltpu.SemaphoreType.REGULAR((max(replicas - 1, 1),))],
        compiler_params=pltpu.CompilerParams(collective_id=0, has_side_effects=True),
    )(values, gate_in, gate_out, cotangent, filters)
    return pl.pallas_call(
        functools.partial(finish, dims),
        out_shape=(
            slab,
            slab,
            slab,
            jax.ShapeDtypeStruct((filter_count // replicas, tokens), f32),
        ),
        in_specs=[vmem] * 5,
        out_specs=(vmem,) * 4,
    )(values, gate_in, cotangent, results, terms)


def body(values, gate_in, gate_out, cotangent, filters):
    seqs, tokens, channels = values.shape
    filter_count = filters.shape[0]
    shards = lax.axis_size("seq")
    replicas = lax.axis_size("batch")
    direct = (
        seqs == 1
        and channels == LANES
        and tokens % LANES == 0
        and channels % filter_count == 0
        and filter_count % (8 * shards) == 0
        and shards % replicas == 0
    )
    chosen = direct_body if direct else spectral_body
    return chosen(values, gate_in, gate_out, cotangent, filters)


def solution(mesh):
    placed = (
        P(None, "seq", "batch"),
        P(None, "seq", "batch"),
        P(None, "seq", "batch"),
        P(None, "seq", "batch"),
        P(None, "seq"),
    )
    return jax.shard_map(
        body,
        mesh=mesh,
        in_specs=placed,
        out_specs=(
            P(None, "seq", "batch"),
            P(None, "seq", "batch"),
            P(None, "seq", "batch"),
            P("batch", "seq"),
        ),
        check_vma=False,
    )
```

```python
import functools
import math

import jax
import jax.numpy as jnp
from jax import lax
from jax.experimental import pallas as pl
from jax.experimental.pallas import tpu as pltpu
from jax.sharding import PartitionSpec as P

HIGHEST = lax.Precision.HIGHEST


def as_sent(x):

    def short(part):
        return part.astype(jnp.bfloat16) if part.dtype == jnp.float32 else part

    return jax.tree.map(short, x)


def angle_table(first, second, period):
    left_idx = lax.broadcasted_iota(jnp.int32, (first, second), 0)
    right_idx = lax.broadcasted_iota(jnp.int32, (first, second), 1)
    angle = (left_idx * right_idx % period).astype(jnp.float32) * (2.0 * math.pi / period)
    return (jnp.cos(angle), jnp.sin(angle))


def dft_tables(used_rows, total_rows, columns):
    modulus = total_rows * columns
    cos_rows, sin_rows = angle_table(total_rows, used_rows, total_rows)
    k_twist = lax.broadcasted_iota(jnp.int32, (total_rows, 1, columns), 0)
    s_twist = lax.broadcasted_iota(jnp.int32, (total_rows, 1, columns), 2)
    angle_twist = (k_twist * s_twist % modulus).astype(jnp.float32) * (2.0 * math.pi / modulus)
    outer_len = max(
        [
            divisor
            for divisor in range(1, columns + 1)
            if columns % divisor == 0 and divisor * divisor <= columns
        ]
    )
    inner_len = columns // outer_len
    cos_outer, sin_outer = angle_table(outer_len, outer_len, outer_len)
    cos_inner, sin_inner = angle_table(inner_len, inner_len, inner_len)
    cos_small, sin_small = angle_table(outer_len, inner_len, columns)
    return (
        cos_rows,
        sin_rows,
        jnp.cos(angle_twist),
        jnp.sin(angle_twist),
        cos_outer,
        sin_outer,
        cos_inner,
        sin_inner,
        cos_small,
        sin_small,
        outer_len,
        inner_len,
        modulus,
    )


def by_rows(table, series):
    return jnp.einsum("kr,rcs->kcs", table, series, precision=HIGHEST)


def to_rows(table, series):
    return jnp.einsum("kr,kcs->rcs", table, series, precision=HIGHEST)


def by_outer(table, series):
    return jnp.einsum("ji,kcis->kcjs", table, series, precision=HIGHEST)


def by_inner(series, table):
    return jnp.einsum("kcjs,sq->kcjq", series, table, precision=HIGHEST)


def inner_forward(part_re, part_im, tables):
    cos_outer, sin_outer, cos_inner, sin_inner, cos_small, sin_small, outer_len, inner_len = tables[
        4:12
    ]
    shape = part_re.shape
    split_re = part_re.reshape(shape[0], shape[1], outer_len, inner_len)
    split_im = part_im.reshape(shape[0], shape[1], outer_len, inner_len)
    first_re = by_outer(cos_outer, split_re) + by_outer(sin_outer, split_im)
    first_im = by_outer(cos_outer, split_im) - by_outer(sin_outer, split_re)
    turned_re = first_re * cos_small + first_im * sin_small
    turned_im = first_im * cos_small - first_re * sin_small
    out_re = by_inner(turned_re, cos_inner) + by_inner(turned_im, sin_inner)
    out_im = by_inner(turned_im, cos_inner) - by_inner(turned_re, sin_inner)
    return (out_re.reshape(shape), out_im.reshape(shape))


def inner_inverse(part_re, part_im, tables):
    cos_outer, sin_outer, cos_inner, sin_inner, cos_small, sin_small, outer_len, inner_len = tables[
        4:12
    ]
    shape = part_re.shape
    split_re = part_re.reshape(shape[0], shape[1], outer_len, inner_len)
    split_im = part_im.reshape(shape[0], shape[1], outer_len, inner_len)
    first_re = by_inner(split_re, cos_inner) - by_inner(split_im, sin_inner)
    first_im = by_inner(split_im, cos_inner) + by_inner(split_re, sin_inner)
    turned_re = first_re * cos_small - first_im * sin_small
    turned_im = first_im * cos_small + first_re * sin_small
    out_re = by_outer(cos_outer, turned_re) - by_outer(sin_outer, turned_im)
    out_im = by_outer(cos_outer, turned_im) + by_outer(sin_outer, turned_re)
    return (out_re.reshape(shape), out_im.reshape(shape))


def spectrum(series, tables):
    cos_rows, sin_rows, cos_twist, sin_twist = tables[0:4]
    first_re = by_rows(cos_rows, series)
    first_im = -by_rows(sin_rows, series)
    turned_re = first_re * cos_twist + first_im * sin_twist
    turned_im = first_im * cos_twist - first_re * sin_twist
    return inner_forward(turned_re, turned_im, tables)


def synthesis(spec_re, spec_im, tables):
    cos_rows, sin_rows, cos_twist, sin_twist = tables[0:4]
    modulus = tables[12]
    inner_re, inner_im = inner_inverse(spec_re, spec_im, tables)
    turned_re = inner_re * cos_twist - inner_im * sin_twist
    turned_im = inner_im * cos_twist + inner_re * sin_twist
    result = to_rows(cos_rows, turned_re) - to_rows(sin_rows, turned_im)
    return result * (1.0 / modulus)


def to_owner(block):
    return jnp.swapaxes(block, 1, 2)[None]


def from_owner(block):
    return jnp.swapaxes(block[0], 1, 2)


def times_bf16(left, right):
    return (left.astype(jnp.float32) * right.astype(jnp.float32)).astype(jnp.bfloat16)


def spectral_body(values, gate_in, gate_out, cotangent, filters):
    seq_count = values.shape[0]
    tokens = values.shape[1]
    channels = values.shape[2]
    filter_count = filters.shape[0]
    shards = lax.axis_size("seq")
    replicas = lax.axis_size("batch")
    owned_count = channels // shards
    tables = dft_tables(shards, 2 * shards, tokens)

    def flatten_series(block):
        return block.reshape(block.shape[0], seq_count * owned_count, tokens)

    def grouped(block):
        return block.reshape(block.shape[0], seq_count, owned_count, tokens)

    spread = jnp.tile(filters, (channels // filter_count, 1)).reshape(1, channels, tokens)
    owned_taps = lax.all_to_all(spread, "seq", split_axis=1, concat_axis=0, tiled=True)
    tap_re, tap_im = spectrum(owned_taps, tables)
    tap_re = tap_re[:, None]
    tap_im = tap_im[:, None]
    mixed_in = times_bf16(values, gate_in)
    grad_mixed = times_bf16(cotangent, gate_out)
    owned_in, owned_grad = (
        lax.all_to_all(to_owner(mixed_in), "seq", split_axis=2, concat_axis=0, tiled=True),
        lax.all_to_all(to_owner(grad_mixed), "seq", split_axis=2, concat_axis=0, tiled=True),
    )
    in_re, in_im = spectrum(flatten_series(owned_in).astype(jnp.float32), tables)
    grad_re, grad_im = spectrum(flatten_series(owned_grad).astype(jnp.float32), tables)
    in_re = grouped(in_re)
    in_im = grouped(in_im)
    grad_re = grouped(grad_re)
    grad_im = grouped(grad_im)
    conv_out = grouped(
        synthesis(
            flatten_series(tap_re * in_re - tap_im * in_im),
            flatten_series(tap_re * in_im + tap_im * in_re),
            tables,
        )
    ).astype(jnp.bfloat16)
    grad_conv_in = grouped(
        synthesis(
            flatten_series(tap_re * grad_re + tap_im * grad_im),
            flatten_series(tap_re * grad_im - tap_im * grad_re),
            tables,
        )
    ).astype(jnp.bfloat16)
    tap_terms = synthesis(
        jnp.sum(in_re * grad_re + in_im * grad_im, axis=1),
        jnp.sum(in_re * grad_im - in_im * grad_re, axis=1),
        tables,
    )
    back_owned, conv_owned = (
        lax.all_to_all(grad_conv_in, "seq", split_axis=0, concat_axis=2, tiled=True),
        lax.all_to_all(conv_out, "seq", split_axis=0, concat_axis=2, tiled=True),
    )
    back_seq = from_owner(back_owned)
    conv_seq = from_owner(conv_owned)
    grad_values = times_bf16(gate_in, back_seq)
    grad_gate_in = times_bf16(values, back_seq)
    grad_gate_out = times_bf16(cotangent, conv_seq)
    tap_seq = lax.all_to_all(
        as_sent(tap_terms), "seq", split_axis=0, concat_axis=1, tiled=True
    ).astype(tap_terms.dtype)
    shared = channels * replicas // filter_count
    factor = 1.0 / math.sqrt(shared * seq_count * shards * tokens)
    per_filter = (
        tap_seq.reshape(channels // filter_count, filter_count, tokens).sum(axis=0) * factor
    )
    grad_filters = lax.psum_scatter(
        per_filter.astype(jnp.bfloat16), "batch", scatter_dimension=0, tiled=True
    ).astype(jnp.float32)
    return (grad_values, grad_gate_in, grad_gate_out, grad_filters)


LANES = 128
SHIFTS = 4
BANKS = 4
MESH = pl.DeviceIdType.MESH


def kernel(
    dims,
    values_ref,
    gate_in_ref,
    gate_out_ref,
    cotangent_ref,
    filters_ref,
    result_held,
    tap_held,
    values_here,
    gate_in_here,
    gate_out_here,
    cotangent_here,
    sent,
    held,
    held_taps,
    taps_rows,
    series,
    padded,
    shifted,
    carried,
    result,
    result_sent,
    tap_rows,
    tap_sent,
    own_sem,
    in_send,
    in_recv,
    taps_send,
    taps_recv,
    out_send,
    out_recv,
    term_send,
    term_recv,
    load_sem,
    near,
):
    shards, replicas, tokens, own, reps, factor = dims
    halves = tokens // LANES
    blocks = shards * halves
    lines = 2 * reps * own
    group = own * shards
    me = lax.axis_index("seq")
    row = lax.axis_index("batch")
    f32, bf16 = jnp.float32, jnp.bfloat16

    barrier = pltpu.get_barrier_semaphore()
    if shards & (shards - 1) == 0:
        digits = [1 << at for at in range(shards.bit_length() - 1)]
        flips = {digit: digit - 2 * digit * lax.rem(me // digit, 2) for digit in digits}
        peers = [
            me + sum(flips[digit] for digit in digits if mask & digit)
            for mask in range(shards - 1, 0, -1)
        ]
    else:
        peers = [lax.rem(me + step, shards) for step in range(1, shards)]
    for peer in peers:
        pl.semaphore_signal(barrier, inc=1, device_id={"seq": peer}, device_id_type=MESH)
    has_below = row > 0
    has_above = row < replicas - 1
    neighbours = has_below.astype(jnp.int32) + has_above.astype(jnp.int32)

    def greet(semaphore):
        @pl.when(has_below)
        def _():
            pl.semaphore_signal(semaphore, inc=1, device_id={"batch": row - 1}, device_id_type=MESH)

        @pl.when(has_above)
        def _():
            pl.semaphore_signal(semaphore, inc=1, device_id={"batch": row + 1}, device_id_type=MESH)

    greet(barrier)
    loads = [
        pltpu.make_async_copy(source, here, load_sem.at[at])
        for at, (source, here) in enumerate(
            (
                (values_ref, values_here),
                (gate_in_ref, gate_in_here),
                (cotangent_ref, cotangent_here),
                (gate_out_ref, gate_out_here),
            )
        )
    ]
    for load in loads:
        load.start()

    down = lax.broadcasted_iota(jnp.int32, (LANES, LANES), 0)
    across = lax.broadcasted_iota(jnp.int32, (LANES, LANES), 1)
    later = across >= down
    mirror = jnp.where(down + across == LANES - 1, 1.0, 0.0).astype(bf16)

    def product(left, right):
        return (left.astype(f32) * right.astype(f32)).astype(bf16)

    for load in loads:
        load.wait()
    for half in range(halves):
        rows = pl.ds(half * LANES, LANES)
        mixed = product(values_here[0, rows, :], gate_in_here[0, rows, :])
        grad = product(cotangent_here[0, rows, :], gate_out_here[0, rows, :])
        mixed_t = mixed.astype(f32).T
        grad_t = jnp.dot(mirror, grad, preferred_element_type=f32).T
        for owner in range(shards):
            parts = [
                part[rep * group + owner * own : rep * group + (owner + 1) * own]
                for part in (mixed_t, grad_t)
                for rep in range(reps)
            ]
            sent[owner, half * lines : (half + 1) * lines, :] = jnp.concatenate(parts, 0).astype(bf16)

    pl.semaphore_wait(barrier, shards - 1 + neighbours)
    if replicas > 1:
        greet(near.at[0])

    def taps_copy(source_owner, slot, peer):
        return pltpu.make_async_remote_copy(
            src_ref=filters_ref.at[pl.ds(pl.multiple_of(source_owner * own, own), own), :],
            dst_ref=held_taps.at[slot],
            send_sem=taps_send.at[peer],
            recv_sem=taps_recv.at[slot],
            device_id={"seq": peer},
            device_id_type=MESH,
        )

    def in_copy(source_owner, slot, peer):
        return pltpu.make_async_remote_copy(
            src_ref=sent.at[source_owner],
            dst_ref=held.at[slot],
            send_sem=in_send.at[peer],
            recv_sem=in_recv.at[slot],
            device_id={"seq": peer},
            device_id_type=MESH,
        )

    def out_copy(slot, peer):
        return pltpu.make_async_remote_copy(
            src_ref=result_sent.at[peer],
            dst_ref=result_held.at[slot],
            send_sem=out_send.at[peer],
            recv_sem=out_recv.at[slot],
            device_id={"seq": peer},
            device_id_type=MESH,
        )

    for peer in peers:
        in_copy(peer, me, peer).start()
    own_in = pltpu.make_async_copy(sent.at[me], held.at[me], own_sem.at[0])
    own_in.start()
    for peer in peers:
        taps_copy(peer, me, peer).start()
    own_taps = pltpu.make_async_copy(
        filters_ref.at[pl.ds(pl.multiple_of(me * own, own), own), :], held_taps.at[me], own_sem.at[1]
    )
    own_taps.start()
    zero_rows = jnp.zeros((blocks, LANES), f32)
    for bank in range(BANKS):
        for rep in range(reps):
            padded[bank, rep, 0:blocks, :] = zero_rows
            padded[bank, reps + rep, blocks : 2 * blocks, :] = zero_rows
    for hop in range(1, min(2, replicas - 1)):
        pl.semaphore_wait(near.at[hop - 1], neighbours)
        greet(near.at[hop])
    own_in.wait()
    for peer in peers:
        in_copy(peer, peer, peer).wait_recv()
    for hop in range(2, replicas - 1):
        pl.semaphore_wait(near.at[hop - 1], neighbours)
        greet(near.at[hop])
    for source in range(shards):
        series[source * halves * lines : (source + 1) * halves * lines, :] = held[source].astype(f32)

    def place(f, padded):
        for line in range(2 * reps):
            at = 0 if line >= reps else blocks
            padded[line, at : at + blocks, :] = series[pl.ds(line * own + f, blocks, stride=lines), :]

    fine = LANES // SHIFTS
    later_fine = later[:fine]
    for bank in range(BANKS):
        carried[bank, 0:8, :] = jnp.zeros((8, LANES), f32)

    def one_gram(f, padded, shifted, carried):
        place(f, padded)
        grad_cols = jnp.concatenate(
            [padded[reps + rep, 0:blocks, :] for rep in range(reps)], 0
        ).T
        grad_cols = jnp.concatenate(
            [grad_cols[shift * fine : (shift + 1) * fine] for shift in range(SHIFTS)], 1
        ).astype(bf16)
        for shift in range(1, SHIFTS):
            for rep in range(reps):
                turned = pltpu.roll(padded[rep], shift * fine, 1)
                carried[8 : 8 + 2 * blocks, :] = turned
                wide = lax.broadcasted_iota(jnp.int32, turned.shape, 1) >= shift * fine
                shifted[(shift - 1) * reps + rep] = jnp.where(
                    wide, turned, carried[7 : 7 + 2 * blocks, :]
                )
        gram_before = None
        for pair in range(blocks // 2):
            left = jnp.concatenate(
                [
                    jnp.concatenate(
                        [padded[rep, blocks - k : 2 * blocks - k, :] for rep in range(reps)]
                        + [
                            shifted[at, blocks - k : 2 * blocks - k, :]
                            for at in range((SHIFTS - 1) * reps)
                        ],
                        0,
                    ).astype(bf16)
                    for k in (2 * pair, 2 * pair + 1)
                ],
                1,
            )
            gram = jnp.dot(grad_cols, left, preferred_element_type=f32)
            for at in range(2):
                k = 2 * pair + at
                gram_now = pltpu.roll(
                    gram[:, at * LANES : (at + 1) * LANES], 0, 1, stride=1, stride_axis=0
                )
                if k > 0:
                    tap_rows[pl.ds((k - 1) * own + f, 1), :] = jnp.sum(
                        jnp.where(later_fine, gram_before, gram_now), axis=0, keepdims=True
                    )
                gram_before = gram_now
        tap_rows[pl.ds((blocks - 1) * own + f, 1), :] = jnp.sum(
            jnp.where(later_fine, gram_before, 0.0), axis=0, keepdims=True
        )

    @pl.loop(0, own // BANKS)
    def _(at):
        for bank in range(BANKS):
            one_gram(at * BANKS + bank, padded.at[bank], shifted.at[bank], carried.at[bank])


    terms = jnp.dot(tap_rows[...].astype(bf16), mirror, preferred_element_type=f32).astype(bf16)
    for peer in range(shards):
        tap_sent[peer] = terms[peer * halves * own : (peer + 1) * halves * own]

    per_row = shards // replicas
    goal = me // per_row
    slot_here = lax.rem(me, per_row) * replicas + row

    def term_copy(peer, to_row, slot):
        return pltpu.make_async_remote_copy(
            src_ref=tap_sent.at[peer],
            dst_ref=tap_held.at[slot],
            send_sem=term_send.at[peer],
            recv_sem=term_recv.at[slot],
            device_id={"seq": peer, "batch": to_row},
            device_id_type=MESH,
        )

    own_term = pltpu.make_async_copy(tap_sent.at[me], tap_held.at[slot_here], own_sem.at[2])
    stays = goal == row
    if replicas > 1:
        pl.semaphore_wait(near.at[replicas - 2], neighbours)
    for peer in peers:
        term_copy(peer, goal, slot_here).start()

    @pl.when(stays)
    def _():
        own_term.start()

    @pl.when(jnp.logical_not(stays))
    def _():
        term_copy(me, goal, slot_here).start()

    own_taps.wait()
    for peer in peers:
        taps_copy(peer, peer, peer).wait_recv()
    for source in range(shards):
        for half in range(halves):
            k = source * halves + half
            taps_rows[k * own : (k + 1) * own, :] = held_taps[
                source, :, half * LANES : (half + 1) * LANES
            ]

    def one_filter(f, padded):
        place(f, padded)
        total = jnp.zeros((2 * reps * blocks, LANES), f32)
        turned_before = jnp.zeros((LANES, LANES), f32)
        for pair in range(blocks // 2):
            lefts, rights = [], []
            for k in (2 * pair, 2 * pair + 1):
                taps = jnp.tile(taps_rows[pl.ds(k * own + f, 8, stride=0), :], (LANES // 8, 1))
                turned = pltpu.roll(taps, 0, 1, stride=1, stride_axis=0)
                rights.append(jnp.where(later, turned, turned_before).astype(bf16))
                turned_before = turned
                lefts.append(
                    jnp.concatenate(
                        [padded[rep, blocks - k : 2 * blocks - k, :] for rep in range(reps)]
                        + [padded[reps + rep, k : blocks + k, :] for rep in range(reps)],
                        0,
                    ).astype(bf16)
                )
            total = total + jnp.dot(
                jnp.concatenate(lefts, 1),
                jnp.concatenate(rights, 0),
                preferred_element_type=f32,
            )
        for line in range(2 * reps):
            result[pl.ds(line * own + f, blocks, stride=lines), :] = total[
                line * blocks : (line + 1) * blocks
            ]

    @pl.loop(0, own // BANKS)
    def _(at):
        for bank in range(BANKS):
            one_filter(at * BANKS + bank, padded.at[bank])


    for peer in range(shards):
        result_sent[peer] = result[
            peer * halves * lines : (peer + 1) * halves * lines, :
        ].astype(bf16)
    for peer in peers:
        out_copy(me, peer).start()
    own_out = pltpu.make_async_copy(result_sent.at[me], result_held.at[me], own_sem.at[0])
    own_out.start()
    own_out.wait()
    for peer in peers:
        out_copy(peer, peer).wait_recv()

    for at in range(per_row):
        for source_row in range(replicas):
            slot = at * replicas + source_row
            local = jnp.logical_and(me == row * per_row + at, row == source_row)

            @pl.when(local)
            def _():
                own_term.wait()

            @pl.when(jnp.logical_not(local))
            def _(slot=slot):
                term_copy(me, row, slot).wait_recv()

    for peer in peers:
        taps_copy(peer, me, peer).wait_send()
        in_copy(peer, me, peer).wait_send()
        out_copy(me, peer).wait_send()
        term_copy(peer, goal, slot_here).wait_send()

    @pl.when(jnp.logical_not(stays))
    def _():
        term_copy(me, goal, slot_here).wait_send()


def finish(
    dims,
    values_ref,
    gate_in_ref,
    cotangent_ref,
    result_held,
    tap_held,
    grad_values_ref,
    grad_gate_in_ref,
    grad_gate_out_ref,
    grad_filters_ref,
):
    shards, replicas, tokens, own, reps, factor = dims
    halves = tokens // LANES
    lines = 2 * reps * own
    f32, bf16 = jnp.float32, jnp.bfloat16
    down = lax.broadcasted_iota(jnp.int32, (LANES, LANES), 0)
    across = lax.broadcasted_iota(jnp.int32, (LANES, LANES), 1)
    mirror = jnp.where(down + across == LANES - 1, 1.0, 0.0).astype(bf16)
    for half in range(halves):
        rows = pl.ds(half * LANES, LANES)
        moved = []
        for kind in range(2):
            at = half * lines + kind * reps * own
            block = jnp.concatenate(
                [
                    result_held[source, at + rep * own : at + (rep + 1) * own, :].astype(f32)
                    for rep in range(reps)
                    for source in range(shards)
                ],
                0,
            )
            moved.append(block.T)
        conv = moved[0]
        back = jnp.dot(mirror, moved[1].astype(bf16), preferred_element_type=f32)
        grad_values_ref[0, rows, :] = (gate_in_ref[0, rows, :].astype(f32) * back).astype(bf16)
        grad_gate_in_ref[0, rows, :] = (values_ref[0, rows, :].astype(f32) * back).astype(bf16)
        grad_gate_out_ref[0, rows, :] = (cotangent_ref[0, rows, :].astype(f32) * conv).astype(bf16)
    for at in range(shards // replicas):
        summed = sum(
            tap_held[at * replicas + source_row].astype(f32) for source_row in range(replicas)
        )
        for half in range(halves):
            grad_filters_ref[at * own : (at + 1) * own, half * LANES : (half + 1) * LANES] = (
                summed[half * own : (half + 1) * own] * factor
            )


def direct_body(values, gate_in, gate_out, cotangent, filters):
    tokens, channels = values.shape[1:]
    filter_count = filters.shape[0]
    shards = lax.axis_size("seq")
    replicas = lax.axis_size("batch")
    own = filter_count // shards
    reps = channels // filter_count
    halves = tokens // LANES
    blocks = shards * halves
    lines = 2 * reps * own
    factor = 1.0 / math.sqrt(reps * replicas * shards * tokens)
    vmem = pl.BlockSpec(memory_space=pltpu.VMEM)
    anywhere = pl.BlockSpec(memory_space=pl.ANY)
    f32, bf16 = jnp.float32, jnp.bfloat16
    slab = jax.ShapeDtypeStruct(values.shape, bf16)
    sems = pltpu.SemaphoreType.DMA((shards,))
    dims = (shards, replicas, tokens, own, reps, factor)
    message = (shards, halves * lines, LANES)
    results, terms = pl.pallas_call(
        functools.partial(kernel, dims),
        out_shape=(
            jax.ShapeDtypeStruct(message, bf16),
            jax.ShapeDtypeStruct((shards, halves * own, LANES), bf16),
        ),
        in_specs=[anywhere] * 5,
        out_specs=(anywhere,) * 2,
        scratch_shapes=[pltpu.VMEM(values.shape, bf16)] * 4
        + [
            pltpu.VMEM(message, bf16),
            pltpu.VMEM(message, bf16),
            pltpu.VMEM((shards, own, tokens), f32),
            pltpu.VMEM((blocks * own + 8, LANES), f32),
            pltpu.VMEM((blocks * lines, LANES), f32),
            pltpu.VMEM((BANKS, 2 * reps, 2 * blocks, LANES), f32),
            pltpu.VMEM((BANKS, (SHIFTS - 1) * reps, 2 * blocks, LANES), f32),
            pltpu.VMEM((BANKS, 8 + 2 * blocks, LANES), f32),
            pltpu.VMEM((blocks * lines, LANES), f32),
            pltpu.VMEM(message, bf16),
            pltpu.VMEM((blocks * own, LANES), f32),
            pltpu.VMEM((shards, halves * own, LANES), bf16),
            pltpu.SemaphoreType.DMA((3,)),
        ]
        + [sems] * 8
        + [pltpu.SemaphoreType.DMA((4,)), pltpu.SemaphoreType.REGULAR((max(replicas - 1, 1),))],
        compiler_params=pltpu.CompilerParams(collective_id=0, has_side_effects=True),
    )(values, gate_in, gate_out, cotangent, filters)
    return pl.pallas_call(
        functools.partial(finish, dims),
        out_shape=(
            slab,
            slab,
            slab,
            jax.ShapeDtypeStruct((filter_count // replicas, tokens), f32),
        ),
        in_specs=[vmem] * 5,
        out_specs=(vmem,) * 4,
    )(values, gate_in, cotangent, results, terms)


def body(values, gate_in, gate_out, cotangent, filters):
    seqs, tokens, channels = values.shape
    filter_count = filters.shape[0]
    shards = lax.axis_size("seq")
    replicas = lax.axis_size("batch")
    direct = (
        seqs == 1
        and channels == LANES
        and tokens % LANES == 0
        and channels % filter_count == 0
        and filter_count % (8 * shards) == 0
        and shards % replicas == 0
    )
    chosen = direct_body if direct else spectral_body
    return chosen(values, gate_in, gate_out, cotangent, filters)


def solution(mesh):
    placed = (
        P(None, "seq", "batch"),
        P(None, "seq", "batch"),
        P(None, "seq", "batch"),
        P(None, "seq", "batch"),
        P(None, "seq"),
    )
    return jax.shard_map(
        body,
        mesh=mesh,
        in_specs=placed,
        out_specs=(
            P(None, "seq", "batch"),
            P(None, "seq", "batch"),
            P(None, "seq", "batch"),
            P("batch", "seq"),
        ),
        check_vma=False,
    )
```

```python
import functools
import math

import jax
import jax.numpy as jnp
from jax import lax
from jax.experimental import pallas as pl
from jax.experimental.pallas import tpu as pltpu
from jax.sharding import PartitionSpec as P

HIGHEST = lax.Precision.HIGHEST


def as_sent(x):

    def short(part):
        return part.astype(jnp.bfloat16) if part.dtype == jnp.float32 else part

    return jax.tree.map(short, x)


def angle_table(first, second, period):
    left_idx = lax.broadcasted_iota(jnp.int32, (first, second), 0)
    right_idx = lax.broadcasted_iota(jnp.int32, (first, second), 1)
    angle = (left_idx * right_idx % period).astype(jnp.float32) * (2.0 * math.pi / period)
    return (jnp.cos(angle), jnp.sin(angle))


def dft_tables(used_rows, total_rows, columns):
    modulus = total_rows * columns
    cos_rows, sin_rows = angle_table(total_rows, used_rows, total_rows)
    k_twist = lax.broadcasted_iota(jnp.int32, (total_rows, 1, columns), 0)
    s_twist = lax.broadcasted_iota(jnp.int32, (total_rows, 1, columns), 2)
    angle_twist = (k_twist * s_twist % modulus).astype(jnp.float32) * (2.0 * math.pi / modulus)
    outer_len = max(
        [
            divisor
            for divisor in range(1, columns + 1)
            if columns % divisor == 0 and divisor * divisor <= columns
        ]
    )
    inner_len = columns // outer_len
    cos_outer, sin_outer = angle_table(outer_len, outer_len, outer_len)
    cos_inner, sin_inner = angle_table(inner_len, inner_len, inner_len)
    cos_small, sin_small = angle_table(outer_len, inner_len, columns)
    return (
        cos_rows,
        sin_rows,
        jnp.cos(angle_twist),
        jnp.sin(angle_twist),
        cos_outer,
        sin_outer,
        cos_inner,
        sin_inner,
        cos_small,
        sin_small,
        outer_len,
        inner_len,
        modulus,
    )


def by_rows(table, series):
    return jnp.einsum("kr,rcs->kcs", table, series, precision=HIGHEST)


def to_rows(table, series):
    return jnp.einsum("kr,kcs->rcs", table, series, precision=HIGHEST)


def by_outer(table, series):
    return jnp.einsum("ji,kcis->kcjs", table, series, precision=HIGHEST)


def by_inner(series, table):
    return jnp.einsum("kcjs,sq->kcjq", series, table, precision=HIGHEST)


def inner_forward(part_re, part_im, tables):
    cos_outer, sin_outer, cos_inner, sin_inner, cos_small, sin_small, outer_len, inner_len = tables[
        4:12
    ]
    shape = part_re.shape
    split_re = part_re.reshape(shape[0], shape[1], outer_len, inner_len)
    split_im = part_im.reshape(shape[0], shape[1], outer_len, inner_len)
    first_re = by_outer(cos_outer, split_re) + by_outer(sin_outer, split_im)
    first_im = by_outer(cos_outer, split_im) - by_outer(sin_outer, split_re)
    turned_re = first_re * cos_small + first_im * sin_small
    turned_im = first_im * cos_small - first_re * sin_small
    out_re = by_inner(turned_re, cos_inner) + by_inner(turned_im, sin_inner)
    out_im = by_inner(turned_im, cos_inner) - by_inner(turned_re, sin_inner)
    return (out_re.reshape(shape), out_im.reshape(shape))


def inner_inverse(part_re, part_im, tables):
    cos_outer, sin_outer, cos_inner, sin_inner, cos_small, sin_small, outer_len, inner_len = tables[
        4:12
    ]
    shape = part_re.shape
    split_re = part_re.reshape(shape[0], shape[1], outer_len, inner_len)
    split_im = part_im.reshape(shape[0], shape[1], outer_len, inner_len)
    first_re = by_inner(split_re, cos_inner) - by_inner(split_im, sin_inner)
    first_im = by_inner(split_im, cos_inner) + by_inner(split_re, sin_inner)
    turned_re = first_re * cos_small - first_im * sin_small
    turned_im = first_im * cos_small + first_re * sin_small
    out_re = by_outer(cos_outer, turned_re) - by_outer(sin_outer, turned_im)
    out_im = by_outer(cos_outer, turned_im) + by_outer(sin_outer, turned_re)
    return (out_re.reshape(shape), out_im.reshape(shape))


def spectrum(series, tables):
    cos_rows, sin_rows, cos_twist, sin_twist = tables[0:4]
    first_re = by_rows(cos_rows, series)
    first_im = -by_rows(sin_rows, series)
    turned_re = first_re * cos_twist + first_im * sin_twist
    turned_im = first_im * cos_twist - first_re * sin_twist
    return inner_forward(turned_re, turned_im, tables)


def synthesis(spec_re, spec_im, tables):
    cos_rows, sin_rows, cos_twist, sin_twist = tables[0:4]
    modulus = tables[12]
    inner_re, inner_im = inner_inverse(spec_re, spec_im, tables)
    turned_re = inner_re * cos_twist - inner_im * sin_twist
    turned_im = inner_im * cos_twist + inner_re * sin_twist
    result = to_rows(cos_rows, turned_re) - to_rows(sin_rows, turned_im)
    return result * (1.0 / modulus)


def to_owner(block):
    return jnp.swapaxes(block, 1, 2)[None]


def from_owner(block):
    return jnp.swapaxes(block[0], 1, 2)


def times_bf16(left, right):
    return (left.astype(jnp.float32) * right.astype(jnp.float32)).astype(jnp.bfloat16)


def spectral_body(values, gate_in, gate_out, cotangent, filters):
    seq_count = values.shape[0]
    tokens = values.shape[1]
    channels = values.shape[2]
    filter_count = filters.shape[0]
    shards = lax.axis_size("seq")
    replicas = lax.axis_size("batch")
    owned_count = channels // shards
    tables = dft_tables(shards, 2 * shards, tokens)

    def flatten_series(block):
        return block.reshape(block.shape[0], seq_count * owned_count, tokens)

    def grouped(block):
        return block.reshape(block.shape[0], seq_count, owned_count, tokens)

    spread = jnp.tile(filters, (channels // filter_count, 1)).reshape(1, channels, tokens)
    owned_taps = lax.all_to_all(spread, "seq", split_axis=1, concat_axis=0, tiled=True)
    tap_re, tap_im = spectrum(owned_taps, tables)
    tap_re = tap_re[:, None]
    tap_im = tap_im[:, None]
    mixed_in = times_bf16(values, gate_in)
    grad_mixed = times_bf16(cotangent, gate_out)
    owned_in, owned_grad = (
        lax.all_to_all(to_owner(mixed_in), "seq", split_axis=2, concat_axis=0, tiled=True),
        lax.all_to_all(to_owner(grad_mixed), "seq", split_axis=2, concat_axis=0, tiled=True),
    )
    in_re, in_im = spectrum(flatten_series(owned_in).astype(jnp.float32), tables)
    grad_re, grad_im = spectrum(flatten_series(owned_grad).astype(jnp.float32), tables)
    in_re = grouped(in_re)
    in_im = grouped(in_im)
    grad_re = grouped(grad_re)
    grad_im = grouped(grad_im)
    conv_out = grouped(
        synthesis(
            flatten_series(tap_re * in_re - tap_im * in_im),
            flatten_series(tap_re * in_im + tap_im * in_re),
            tables,
        )
    ).astype(jnp.bfloat16)
    grad_conv_in = grouped(
        synthesis(
            flatten_series(tap_re * grad_re + tap_im * grad_im),
            flatten_series(tap_re * grad_im - tap_im * grad_re),
            tables,
        )
    ).astype(jnp.bfloat16)
    tap_terms = synthesis(
        jnp.sum(in_re * grad_re + in_im * grad_im, axis=1),
        jnp.sum(in_re * grad_im - in_im * grad_re, axis=1),
        tables,
    )
    back_owned, conv_owned = (
        lax.all_to_all(grad_conv_in, "seq", split_axis=0, concat_axis=2, tiled=True),
        lax.all_to_all(conv_out, "seq", split_axis=0, concat_axis=2, tiled=True),
    )
    back_seq = from_owner(back_owned)
    conv_seq = from_owner(conv_owned)
    grad_values = times_bf16(gate_in, back_seq)
    grad_gate_in = times_bf16(values, back_seq)
    grad_gate_out = times_bf16(cotangent, conv_seq)
    tap_seq = lax.all_to_all(
        as_sent(tap_terms), "seq", split_axis=0, concat_axis=1, tiled=True
    ).astype(tap_terms.dtype)
    shared = channels * replicas // filter_count
    factor = 1.0 / math.sqrt(shared * seq_count * shards * tokens)
    per_filter = (
        tap_seq.reshape(channels // filter_count, filter_count, tokens).sum(axis=0) * factor
    )
    grad_filters = lax.psum_scatter(
        per_filter.astype(jnp.bfloat16), "batch", scatter_dimension=0, tiled=True
    ).astype(jnp.float32)
    return (grad_values, grad_gate_in, grad_gate_out, grad_filters)


LANES = 128
SHIFTS = 4
BANKS = 8
MESH = pl.DeviceIdType.MESH


def kernel(
    dims,
    values_ref,
    gate_in_ref,
    gate_out_ref,
    cotangent_ref,
    filters_ref,
    result_held,
    tap_held,
    values_here,
    gate_in_here,
    gate_out_here,
    cotangent_here,
    sent,
    held,
    held_taps,
    taps_rows,
    series,
    padded,
    shifted,
    carried,
    result,
    result_sent,
    tap_rows,
    tap_sent,
    own_sem,
    in_send,
    in_recv,
    taps_send,
    taps_recv,
    out_send,
    out_recv,
    term_send,
    term_recv,
    load_sem,
    near,
):
    shards, replicas, tokens, own, reps, factor = dims
    halves = tokens // LANES
    blocks = shards * halves
    lines = 2 * reps * own
    group = own * shards
    me = lax.axis_index("seq")
    row = lax.axis_index("batch")
    f32, bf16 = jnp.float32, jnp.bfloat16

    barrier = pltpu.get_barrier_semaphore()
    if shards & (shards - 1) == 0:
        digits = [1 << at for at in range(shards.bit_length() - 1)]
        flips = {digit: digit - 2 * digit * lax.rem(me // digit, 2) for digit in digits}
        peers = [
            me + sum(flips[digit] for digit in digits if mask & digit)
            for mask in range(shards - 1, 0, -1)
        ]
    else:
        peers = [lax.rem(me + step, shards) for step in range(1, shards)]
    for peer in peers:
        pl.semaphore_signal(barrier, inc=1, device_id={"seq": peer}, device_id_type=MESH)
    has_below = row > 0
    has_above = row < replicas - 1
    neighbours = has_below.astype(jnp.int32) + has_above.astype(jnp.int32)

    def greet(semaphore):
        @pl.when(has_below)
        def _():
            pl.semaphore_signal(semaphore, inc=1, device_id={"batch": row - 1}, device_id_type=MESH)

        @pl.when(has_above)
        def _():
            pl.semaphore_signal(semaphore, inc=1, device_id={"batch": row + 1}, device_id_type=MESH)

    greet(barrier)
    loads = [
        pltpu.make_async_copy(source, here, load_sem.at[at])
        for at, (source, here) in enumerate(
            (
                (values_ref, values_here),
                (gate_in_ref, gate_in_here),
                (cotangent_ref, cotangent_here),
                (gate_out_ref, gate_out_here),
            )
        )
    ]
    for load in loads:
        load.start()

    down = lax.broadcasted_iota(jnp.int32, (LANES, LANES), 0)
    across = lax.broadcasted_iota(jnp.int32, (LANES, LANES), 1)
    later = across >= down
    mirror = jnp.where(down + across == LANES - 1, 1.0, 0.0).astype(bf16)

    def product(left, right):
        return (left.astype(f32) * right.astype(f32)).astype(bf16)

    for load in loads:
        load.wait()
    for half in range(halves):
        rows = pl.ds(half * LANES, LANES)
        mixed = product(values_here[0, rows, :], gate_in_here[0, rows, :])
        grad = product(cotangent_here[0, rows, :], gate_out_here[0, rows, :])
        mixed_t = mixed.astype(f32).T
        grad_t = jnp.dot(mirror, grad, preferred_element_type=f32).T
        for owner in range(shards):
            parts = [
                part[rep * group + owner * own : rep * group + (owner + 1) * own]
                for part in (mixed_t, grad_t)
                for rep in range(reps)
            ]
            sent[owner, half * lines : (half + 1) * lines, :] = jnp.concatenate(parts, 0).astype(bf16)

    pl.semaphore_wait(barrier, shards - 1 + neighbours)
    if replicas > 1:
        greet(near.at[0])

    def taps_copy(source_owner, slot, peer):
        return pltpu.make_async_remote_copy(
            src_ref=filters_ref.at[pl.ds(pl.multiple_of(source_owner * own, own), own), :],
            dst_ref=held_taps.at[slot],
            send_sem=taps_send.at[peer],
            recv_sem=taps_recv.at[slot],
            device_id={"seq": peer},
            device_id_type=MESH,
        )

    def in_copy(source_owner, slot, peer):
        return pltpu.make_async_remote_copy(
            src_ref=sent.at[source_owner],
            dst_ref=held.at[slot],
            send_sem=in_send.at[peer],
            recv_sem=in_recv.at[slot],
            device_id={"seq": peer},
            device_id_type=MESH,
        )

    def out_copy(slot, peer):
        return pltpu.make_async_remote_copy(
            src_ref=result_sent.at[peer],
            dst_ref=result_held.at[slot],
            send_sem=out_send.at[peer],
            recv_sem=out_recv.at[slot],
            device_id={"seq": peer},
            device_id_type=MESH,
        )

    for peer in peers:
        in_copy(peer, me, peer).start()
    own_in = pltpu.make_async_copy(sent.at[me], held.at[me], own_sem.at[0])
    own_in.start()
    for peer in peers:
        taps_copy(peer, me, peer).start()
    own_taps = pltpu.make_async_copy(
        filters_ref.at[pl.ds(pl.multiple_of(me * own, own), own), :], held_taps.at[me], own_sem.at[1]
    )
    own_taps.start()
    zero_rows = jnp.zeros((blocks, LANES), f32)
    for bank in range(BANKS):
        for rep in range(reps):
            padded[bank, rep, 0:blocks, :] = zero_rows
            padded[bank, reps + rep, blocks : 2 * blocks, :] = zero_rows
    for hop in range(1, min(2, replicas - 1)):
        pl.semaphore_wait(near.at[hop - 1], neighbours)
        greet(near.at[hop])
    own_in.wait()
    for peer in peers:
        in_copy(peer, peer, peer).wait_recv()
    for hop in range(2, replicas - 1):
        pl.semaphore_wait(near.at[hop - 1], neighbours)
        greet(near.at[hop])
    for source in range(shards):
        series[source * halves * lines : (source + 1) * halves * lines, :] = held[source].astype(f32)

    def place(f, padded):
        for line in range(2 * reps):
            at = 0 if line >= reps else blocks
            padded[line, at : at + blocks, :] = series[pl.ds(line * own + f, blocks, stride=lines), :]

    fine = LANES // SHIFTS
    later_fine = later[:fine]
    for bank in range(BANKS):
        carried[bank, 0:8, :] = jnp.zeros((8, LANES), f32)

    def one_gram(f, padded, shifted, carried):
        place(f, padded)
        grad_cols = jnp.concatenate(
            [padded[reps + rep, 0:blocks, :] for rep in range(reps)], 0
        ).T
        grad_cols = jnp.concatenate(
            [grad_cols[shift * fine : (shift + 1) * fine] for shift in range(SHIFTS)], 1
        ).astype(bf16)
        for shift in range(1, SHIFTS):
            for rep in range(reps):
                turned = pltpu.roll(padded[rep], shift * fine, 1)
                carried[8 : 8 + 2 * blocks, :] = turned
                wide = lax.broadcasted_iota(jnp.int32, turned.shape, 1) >= shift * fine
                shifted[(shift - 1) * reps + rep] = jnp.where(
                    wide, turned, carried[7 : 7 + 2 * blocks, :]
                )
        gram_before = None
        for pair in range(blocks // 2):
            left = jnp.concatenate(
                [
                    jnp.concatenate(
                        [padded[rep, blocks - k : 2 * blocks - k, :] for rep in range(reps)]
                        + [
                            shifted[at, blocks - k : 2 * blocks - k, :]
                            for at in range((SHIFTS - 1) * reps)
                        ],
                        0,
                    ).astype(bf16)
                    for k in (2 * pair, 2 * pair + 1)
                ],
                1,
            )
            gram = jnp.dot(grad_cols, left, preferred_element_type=f32)
            for at in range(2):
                k = 2 * pair + at
                gram_now = pltpu.roll(
                    gram[:, at * LANES : (at + 1) * LANES], 0, 1, stride=1, stride_axis=0
                )
                if k > 0:
                    tap_rows[pl.ds((k - 1) * own + f, 1), :] = jnp.sum(
                        jnp.where(later_fine, gram_before, gram_now), axis=0, keepdims=True
                    )
                gram_before = gram_now
        tap_rows[pl.ds((blocks - 1) * own + f, 1), :] = jnp.sum(
            jnp.where(later_fine, gram_before, 0.0), axis=0, keepdims=True
        )

    @pl.loop(0, own // BANKS)
    def _(at):
        for bank in range(BANKS):
            one_gram(at * BANKS + bank, padded.at[bank], shifted.at[bank], carried.at[bank])


    terms = jnp.dot(tap_rows[...].astype(bf16), mirror, preferred_element_type=f32).astype(bf16)
    for peer in range(shards):
        tap_sent[peer] = terms[peer * halves * own : (peer + 1) * halves * own]

    per_row = shards // replicas
    goal = me // per_row
    slot_here = lax.rem(me, per_row) * replicas + row

    def term_copy(peer, to_row, slot):
        return pltpu.make_async_remote_copy(
            src_ref=tap_sent.at[peer],
            dst_ref=tap_held.at[slot],
            send_sem=term_send.at[peer],
            recv_sem=term_recv.at[slot],
            device_id={"seq": peer, "batch": to_row},
            device_id_type=MESH,
        )

    own_term = pltpu.make_async_copy(tap_sent.at[me], tap_held.at[slot_here], own_sem.at[2])
    stays = goal == row
    if replicas > 1:
        pl.semaphore_wait(near.at[replicas - 2], neighbours)
    for peer in peers:
        term_copy(peer, goal, slot_here).start()

    @pl.when(stays)
    def _():
        own_term.start()

    @pl.when(jnp.logical_not(stays))
    def _():
        term_copy(me, goal, slot_here).start()

    own_taps.wait()
    for peer in peers:
        taps_copy(peer, peer, peer).wait_recv()
    for source in range(shards):
        for half in range(halves):
            k = source * halves + half
            taps_rows[k * own : (k + 1) * own, :] = held_taps[
                source, :, half * LANES : (half + 1) * LANES
            ]

    def one_filter(f, padded):
        place(f, padded)
        total = jnp.zeros((2 * reps * blocks, LANES), f32)
        turned_before = jnp.zeros((LANES, LANES), f32)
        for pair in range(blocks // 2):
            lefts, rights = [], []
            for k in (2 * pair, 2 * pair + 1):
                taps = jnp.tile(taps_rows[pl.ds(k * own + f, 8, stride=0), :], (LANES // 8, 1))
                turned = pltpu.roll(taps, 0, 1, stride=1, stride_axis=0)
                rights.append(jnp.where(later, turned, turned_before).astype(bf16))
                turned_before = turned
                lefts.append(
                    jnp.concatenate(
                        [padded[rep, blocks - k : 2 * blocks - k, :] for rep in range(reps)]
                        + [padded[reps + rep, k : blocks + k, :] for rep in range(reps)],
                        0,
                    ).astype(bf16)
                )
            total = total + jnp.dot(
                jnp.concatenate(lefts, 1),
                jnp.concatenate(rights, 0),
                preferred_element_type=f32,
            )
        for line in range(2 * reps):
            result[pl.ds(line * own + f, blocks, stride=lines), :] = total[
                line * blocks : (line + 1) * blocks
            ]

    @pl.loop(0, own // BANKS)
    def _(at):
        for bank in range(BANKS):
            one_filter(at * BANKS + bank, padded.at[bank])


    for peer in range(shards):
        result_sent[peer] = result[
            peer * halves * lines : (peer + 1) * halves * lines, :
        ].astype(bf16)
    for peer in peers:
        out_copy(me, peer).start()
    own_out = pltpu.make_async_copy(result_sent.at[me], result_held.at[me], own_sem.at[0])
    own_out.start()
    own_out.wait()
    for peer in peers:
        out_copy(peer, peer).wait_recv()

    for at in range(per_row):
        for source_row in range(replicas):
            slot = at * replicas + source_row
            local = jnp.logical_and(me == row * per_row + at, row == source_row)

            @pl.when(local)
            def _():
                own_term.wait()

            @pl.when(jnp.logical_not(local))
            def _(slot=slot):
                term_copy(me, row, slot).wait_recv()

    for peer in peers:
        taps_copy(peer, me, peer).wait_send()
        in_copy(peer, me, peer).wait_send()
        out_copy(me, peer).wait_send()
        term_copy(peer, goal, slot_here).wait_send()

    @pl.when(jnp.logical_not(stays))
    def _():
        term_copy(me, goal, slot_here).wait_send()


def finish(
    dims,
    values_ref,
    gate_in_ref,
    cotangent_ref,
    result_held,
    tap_held,
    grad_values_ref,
    grad_gate_in_ref,
    grad_gate_out_ref,
    grad_filters_ref,
):
    shards, replicas, tokens, own, reps, factor = dims
    halves = tokens // LANES
    lines = 2 * reps * own
    f32, bf16 = jnp.float32, jnp.bfloat16
    down = lax.broadcasted_iota(jnp.int32, (LANES, LANES), 0)
    across = lax.broadcasted_iota(jnp.int32, (LANES, LANES), 1)
    mirror = jnp.where(down + across == LANES - 1, 1.0, 0.0).astype(bf16)
    for half in range(halves):
        rows = pl.ds(half * LANES, LANES)
        moved = []
        for kind in range(2):
            at = half * lines + kind * reps * own
            block = jnp.concatenate(
                [
                    result_held[source, at + rep * own : at + (rep + 1) * own, :].astype(f32)
                    for rep in range(reps)
                    for source in range(shards)
                ],
                0,
            )
            moved.append(block.T)
        conv = moved[0]
        back = jnp.dot(mirror, moved[1].astype(bf16), preferred_element_type=f32)
        grad_values_ref[0, rows, :] = (gate_in_ref[0, rows, :].astype(f32) * back).astype(bf16)
        grad_gate_in_ref[0, rows, :] = (values_ref[0, rows, :].astype(f32) * back).astype(bf16)
        grad_gate_out_ref[0, rows, :] = (cotangent_ref[0, rows, :].astype(f32) * conv).astype(bf16)
    for at in range(shards // replicas):
        summed = sum(
            tap_held[at * replicas + source_row].astype(f32) for source_row in range(replicas)
        )
        for half in range(halves):
            grad_filters_ref[at * own : (at + 1) * own, half * LANES : (half + 1) * LANES] = (
                summed[half * own : (half + 1) * own] * factor
            )


def direct_body(values, gate_in, gate_out, cotangent, filters):
    tokens, channels = values.shape[1:]
    filter_count = filters.shape[0]
    shards = lax.axis_size("seq")
    replicas = lax.axis_size("batch")
    own = filter_count // shards
    reps = channels // filter_count
    halves = tokens // LANES
    blocks = shards * halves
    lines = 2 * reps * own
    factor = 1.0 / math.sqrt(reps * replicas * shards * tokens)
    vmem = pl.BlockSpec(memory_space=pltpu.VMEM)
    anywhere = pl.BlockSpec(memory_space=pl.ANY)
    f32, bf16 = jnp.float32, jnp.bfloat16
    slab = jax.ShapeDtypeStruct(values.shape, bf16)
    sems = pltpu.SemaphoreType.DMA((shards,))
    dims = (shards, replicas, tokens, own, reps, factor)
    message = (shards, halves * lines, LANES)
    results, terms = pl.pallas_call(
        functools.partial(kernel, dims),
        out_shape=(
            jax.ShapeDtypeStruct(message, bf16),
            jax.ShapeDtypeStruct((shards, halves * own, LANES), bf16),
        ),
        in_specs=[anywhere] * 5,
        out_specs=(anywhere,) * 2,
        scratch_shapes=[pltpu.VMEM(values.shape, bf16)] * 4
        + [
            pltpu.VMEM(message, bf16),
            pltpu.VMEM(message, bf16),
            pltpu.VMEM((shards, own, tokens), f32),
            pltpu.VMEM((blocks * own + 8, LANES), f32),
            pltpu.VMEM((blocks * lines, LANES), f32),
            pltpu.VMEM((BANKS, 2 * reps, 2 * blocks, LANES), f32),
            pltpu.VMEM((BANKS, (SHIFTS - 1) * reps, 2 * blocks, LANES), f32),
            pltpu.VMEM((BANKS, 8 + 2 * blocks, LANES), f32),
            pltpu.VMEM((blocks * lines, LANES), f32),
            pltpu.VMEM(message, bf16),
            pltpu.VMEM((blocks * own, LANES), f32),
            pltpu.VMEM((shards, halves * own, LANES), bf16),
            pltpu.SemaphoreType.DMA((3,)),
        ]
        + [sems] * 8
        + [pltpu.SemaphoreType.DMA((4,)), pltpu.SemaphoreType.REGULAR((max(replicas - 1, 1),))],
        compiler_params=pltpu.CompilerParams(collective_id=0, has_side_effects=True),
    )(values, gate_in, gate_out, cotangent, filters)
    return pl.pallas_call(
        functools.partial(finish, dims),
        out_shape=(
            slab,
            slab,
            slab,
            jax.ShapeDtypeStruct((filter_count // replicas, tokens), f32),
        ),
        in_specs=[vmem] * 5,
        out_specs=(vmem,) * 4,
    )(values, gate_in, cotangent, results, terms)


def body(values, gate_in, gate_out, cotangent, filters):
    seqs, tokens, channels = values.shape
    filter_count = filters.shape[0]
    shards = lax.axis_size("seq")
    replicas = lax.axis_size("batch")
    direct = (
        seqs == 1
        and channels == LANES
        and tokens % LANES == 0
        and channels % filter_count == 0
        and filter_count % (8 * shards) == 0
        and shards % replicas == 0
    )
    chosen = direct_body if direct else spectral_body
    return chosen(values, gate_in, gate_out, cotangent, filters)


def solution(mesh):
    placed = (
        P(None, "seq", "batch"),
        P(None, "seq", "batch"),
        P(None, "seq", "batch"),
        P(None, "seq", "batch"),
        P(None, "seq"),
    )
    return jax.shard_map(
        body,
        mesh=mesh,
        in_specs=placed,
        out_specs=(
            P(None, "seq", "batch"),
            P(None, "seq", "batch"),
            P(None, "seq", "batch"),
            P("batch", "seq"),
        ),
        check_vma=False,
    )
```
